512 devices in a mesh: group: 16 (over y, x), member: 32 (over z, core).
Axes of the slice: x: 4, y: 4, z: 16, core: 2. Of those that a mesh axis runs over, the one named last changes fastest.
Arguments:
- layer_in: bfloat16 [262144, 512], P(('group', 'member')), may hold values from -6 to 6
- first_layer: bfloat16 [262144, 512], P(('group', 'member')), may hold values from -6 to 6
- weight: bfloat16 [512, 512], replicated, may hold values from -0.25 to 0.25
- tiles: bfloat16 [2048, 10, 128, 128], P(('group', 'member')), may hold values from -0.25 to 0.25
- tile_cols: int32 [2048, 10], P(('group', 'member')), may hold values from 0 to 51, as said below
- tile_count: int32 [2048], P(('group', 'member')), may hold values from 1 to 10, as said below
- history: bfloat16 [131072, 512], P(('group', 'member')), may hold values from -6 to 6
- member_serve: int32 [512, 32], P(('group', 'member')), may hold values from 0 to 1
- group_serve: int32 [512, 16], P(('group', 'member')), may hold values from 0 to 1
- push_pick: int32 [512, 32, 4], P(('group', 'member')), may hold values from 0 to 511
- push_row: int32 [512, 32, 4], P(('group', 'member')), may hold values from 0 to 255, as said below
- cotangent: bfloat16 [262144, 512], P(('group', 'member')), may hold values from -6 to 6
Outputs:
- layer_out: bfloat16 [262144, 512], P(('group', 'member'))
- grad_layer: bfloat16 [262144, 512], P(('group', 'member'))
- grad_weight: bfloat16 [512, 512], replicated
- new_history: bfloat16 [131072, 512], P(('group', 'member'))
The draws below stay inside these ranges and needn't reach their ends.
Inputs may be any that keep to these rules, and one draw needn't show every extreme that they name: `tile_cols`: column c of a block row's tile list names: c < 4, a batch block of the same device; 4 <= c < 36, the block served by member c - 4 of the group; otherwise the block served by group c - 36 at the same member index. Slots at or beyond the block row's count hold arbitrary values. `tile_count`: live slots of a block row. `push_row`: the 128 rows named by one receiving device are distinct.
All inputs are finite; a program needn't handle non-finite values.
Results may differ from the reference program's by a relative error of at most 0.0085.
Values may be sent and summed in bfloat16 or wider, within the bound.
No kernel may reach another device: no remote copies, remote signals or barrier semaphores. Data moves between devices by JAX's collectives and lax.ppermute only.
A program may use at most 64 MiB of HBM per device.

```python
import math
import jax
import jax.numpy as jnp
from jax import lax

D = 512
BLK = 128
NB = 4
TILES = 10
HB = 2
PR = 4
DEVS = 512
NCOL = 52
ROWS = 262144
TILE_ROWS = 2048
HIST_ROWS = 131072
N_GROUP = 16
N_MEMBER = 32


def draw_tile_cols(key, part):
    key_coin = jax.random.fold_in(key, 11)
    key_local = jax.random.fold_in(key, 12)
    key_remote = jax.random.fold_in(key, 13)
    coin = jax.random.randint(key_coin, (TILE_ROWS, TILES), 0, 4)
    local_cols = jax.random.randint(key_local, (TILE_ROWS, TILES), 0, NB)
    remote_cols = jax.random.randint(key_remote, (TILE_ROWS, TILES), NB, NCOL)
    chosen = jnp.where(coin == 0, local_cols, remote_cols)
    chosen = chosen.at[0, 0].set(NCOL - 1)
    chosen = chosen.at[0, 1].set(0)
    return chosen.astype(jnp.int32)


def draw_tile_count(key, part):
    key_heavy = jax.random.fold_in(key, 21)
    key_light = jax.random.fold_in(key, 22)
    key_busy = jax.random.fold_in(key, 23)
    heavy_dev = jax.random.randint(key_heavy, (DEVS, 1), 0, 4) == 0
    light_vals = jax.random.randint(key_light, (DEVS, NB), max(1, 7 * TILES // 10), TILES + 1)
    busy_vals = jax.random.randint(key_busy, (DEVS, NB), max(1, 9 * TILES // 10), TILES + 1)
    counts = jnp.where(heavy_dev, busy_vals, light_vals).reshape(DEVS * NB)
    counts = counts.at[0].set(TILES)
    return counts.astype(jnp.int32)


def draw_push_row(key, part):
    hist_rows = HB * BLK
    taken = N_MEMBER * PR
    keys = jax.random.split(jax.random.fold_in(key, 31), DEVS)

    def one_device(device_key):
        order = jax.random.permutation(device_key, hist_rows)[:taken]
        shift_by = hist_rows - 1 - order[0]
        return (order + shift_by) % hist_rows
    rows = jax.vmap(one_device)(keys)
    return rows.reshape(DEVS, N_MEMBER, PR).astype(jnp.int32)


def set_ends(entries, stream_key, least, largest):
    longest = entries.shape.index(max(entries.shape))
    spots = []
    for shift in (0, 1):
        where = [jax.random.randint(jax.random.fold_in(stream_key, axis), (), 0, length) for axis, length in enumerate(entries.shape)]
        where[longest] = (where[longest] + shift) % entries.shape[longest]
        spots.append(tuple(where))
    return entries.at[spots[0]].set(least).at[spots[1]].set(largest)


def levels(stream_key, dims, pieces, least, high):
    gain = 1.0
    for dim, shards_of in pieces:
        draws = jax.random.uniform(jax.random.fold_in(jax.random.fold_in(stream_key, 6), dim), (shards_of,), jnp.float32, least / len(pieces), high / len(pieces))
        gain = gain * jnp.repeat(jnp.exp(draws), dims[dim] // shards_of).reshape((-1,) + (1,) * (len(dims) - 1 - dim))
    return gain


def bell_draw(stream_key, dims, scale, reach, pieces=(), kind=jnp.bfloat16):
    result = jax.random.normal(stream_key, dims, jnp.float32) * scale
    if len(pieces) > 0:
        result = levels(stream_key, dims, pieces, -0.22, 0.18) * result
    return jnp.clip(result, min=-reach, max=reach).astype(kind)


def setup_inputs(seed: int = 0) -> dict:
    splits = jax.random.split(jax.random.key(seed), 13)
    return {
        "layer_in": bell_draw(splits[0], (ROWS, D), 1.0, 6.0, ((0, 512),)),
        "first_layer": bell_draw(splits[1], (ROWS, D), 1.0, 6.0, ((0, 512),)),
        "weight": bell_draw(splits[2], (D, D), D ** -0.5, 0.25),
        "tiles": bell_draw(splits[3], (TILE_ROWS, TILES, BLK, BLK), (4 * BLK) ** -0.5, 0.25, ((0, 512),)),
        "tile_cols": draw_tile_cols(jax.random.fold_in(splits[12], 71), 0),
        "tile_count": draw_tile_count(jax.random.fold_in(splits[12], 71), 0),
        "history": bell_draw(splits[6], (HIST_ROWS, D), 1.0, 6.0, ((0, 512),)),
        "member_serve": set_ends(jax.random.randint(splits[7], (DEVS, N_MEMBER), 0, HB), jax.random.fold_in(splits[7], 1), 0, HB - 1).astype(jnp.int32),
        "group_serve": set_ends(jax.random.randint(splits[8], (DEVS, N_GROUP), 0, HB), jax.random.fold_in(splits[8], 1), 0, HB - 1).astype(jnp.int32),
        "push_pick": set_ends(jax.random.randint(splits[9], (DEVS, N_MEMBER, PR), 0, NB * BLK), jax.random.fold_in(splits[9], 1), 0, (NB * BLK) - 1).astype(jnp.int32),
        "push_row": draw_push_row(jax.random.fold_in(splits[12], 71), 0),
        "cotangent": bell_draw(splits[11], (ROWS, D), 1.0, 6.0, ((0, 512),)),
    }


alpha_mix = 0.1
beta_map = math.log(1.5)


def combine_tiles(tile_vals, tile_mask, sources, col_index):
    picked = sources[col_index].astype(jnp.float32)
    kept_tiles = jnp.where(tile_mask[:, :, None, None], tile_vals, jnp.zeros_like(tile_vals)).astype(jnp.float32)
    return jnp.einsum("itrk,itkd->ird", kept_tiles, picked)


def reference(layer_in, first_layer, weight, tiles, tile_cols, tile_count, history, member_serve, group_serve, push_pick, push_row, cotangent):
    stored_all = history.reshape(N_GROUP, N_MEMBER, HB, BLK, D)
    serve_member = member_serve.reshape(N_GROUP, N_MEMBER, N_MEMBER)
    serve_group = group_serve.reshape(N_GROUP, N_MEMBER, N_GROUP)
    member_ids = jnp.arange(N_MEMBER, dtype=jnp.int32)
    group_ids = jnp.arange(N_GROUP, dtype=jnp.int32)

    def device_step(grad_total, device):
        group_idx = device // N_MEMBER
        member_idx = device % N_MEMBER
        from_members = stored_all[group_idx][member_ids, serve_member[group_idx, :, member_idx]]
        from_groups = stored_all[group_ids, member_idx, serve_group[:, member_idx, group_idx]]
        row_first = device * (NB * BLK)
        own_blocks = lax.dynamic_slice_in_dim(layer_in, row_first, NB * BLK, 0).reshape(NB, BLK, D)
        columns = jnp.concatenate([own_blocks, from_members, from_groups], axis=0)
        tile_vals = lax.dynamic_slice_in_dim(tiles, device * NB, NB, 0)
        col_index = lax.dynamic_slice_in_dim(tile_cols, device * NB, NB, 0)
        counts_here = lax.dynamic_slice_in_dim(tile_count, device * NB, NB, 0)
        live_tiles = jnp.arange(TILES, dtype=jnp.int32)[None, :] < counts_here[:, None]
        neighbour_sum = combine_tiles(tile_vals, live_tiles, columns, col_index)
        first_rows = lax.dynamic_slice_in_dim(first_layer, row_first, NB * BLK, 0)
        support = ((1.0 - alpha_mix) * neighbour_sum.reshape(NB * BLK, D) + alpha_mix * first_rows.astype(jnp.float32)).astype(jnp.bfloat16)
        mixed_out = jnp.dot(support, weight, preferred_element_type=jnp.float32)
        pre_act = (1.0 - beta_map) * support.astype(jnp.float32) + beta_map * mixed_out
        layer_out = jax.nn.silu(pre_act).astype(jnp.bfloat16)
        sigmoid_pre = jax.nn.sigmoid(pre_act)
        grad_rows = lax.dynamic_slice_in_dim(cotangent, row_first, NB * BLK, 0).astype(jnp.float32)
        grad_pre = (grad_rows * sigmoid_pre * (1.0 + pre_act * (1.0 - sigmoid_pre))).astype(jnp.bfloat16)
        weight_term = jnp.dot(support.T, grad_pre, preferred_element_type=jnp.float32)
        back_term = jnp.dot(grad_pre, weight.T, preferred_element_type=jnp.float32)
        grad_support = ((1.0 - beta_map) * grad_pre.astype(jnp.float32) + beta_map * back_term).astype(jnp.bfloat16)
        local_mask = live_tiles & (col_index < NB)
        kept_tiles = jnp.where(local_mask[:, :, None, None], tile_vals, jnp.zeros_like(tile_vals)).astype(jnp.float32)
        spread = jnp.einsum("itrk,ird->itkd", kept_tiles, grad_support.reshape(NB, BLK, D).astype(jnp.float32))
        owner_hot = (col_index[:, :, None] == jnp.arange(NB, dtype=jnp.int32)[None, None, :]).astype(jnp.float32)
        grad_blocks = jnp.einsum("itj,itkd->jkd", owner_hot, spread)
        grad_layer = ((1.0 - alpha_mix) * grad_blocks).reshape(NB * BLK, D).astype(jnp.bfloat16)
        return grad_total + weight_term, (layer_out, grad_layer)

    grad_total, (outs, grads) = lax.scan(device_step, jnp.zeros((D, D), jnp.float32), jnp.arange(N_GROUP * N_MEMBER, dtype=jnp.int32))
    layer_out = outs.reshape(N_GROUP * N_MEMBER * NB * BLK, D)
    grad_layer = grads.reshape(N_GROUP * N_MEMBER * NB * BLK, D)
    grad_weight = (beta_map * grad_total).astype(jnp.bfloat16)

    out_grid = layer_out.reshape(N_GROUP, N_MEMBER, NB * BLK, D)
    pick_grid = push_pick.reshape(N_GROUP, N_MEMBER, N_MEMBER, PR)
    row_grid = push_row.reshape(N_GROUP, N_MEMBER, N_MEMBER, PR)
    hist_grid = history.reshape(N_GROUP, N_MEMBER, HB * BLK, D)

    def receive(receiver):
        group_idx = receiver // N_MEMBER
        member_idx = receiver % N_MEMBER
        arrived = out_grid[group_idx][member_ids[:, None], pick_grid[group_idx, :, member_idx, :]]
        return hist_grid[group_idx, member_idx].at[row_grid[group_idx, member_idx].reshape(-1)].set(arrived.reshape(-1, D))

    new_history = lax.map(receive, jnp.arange(N_GROUP * N_MEMBER, dtype=jnp.int32)).reshape(N_GROUP * N_MEMBER * HB * BLK, D)
    return (layer_out, grad_layer, grad_weight, new_history)
```

```python
import math

import jax
import jax.numpy as jnp
from jax import lax
from jax.experimental import pallas as pl
from jax.experimental.pallas import tpu as pltpu
from jax.sharding import Mesh, PartitionSpec as P

alpha_mix = 0.1
beta_map = math.log(1.5)

PLANE = ("y", "x", "core")
MEMBER = ("z", "core")
GROUP = ("y", "x")
ALL = ("y", "x", "z", "core")


def exchange(x, axes):
    return lax.all_to_all(x, axes, split_axis=0, concat_axis=0, tiled=True)


def sigmoid(v):
    return 1.0 / (1.0 + jnp.exp(-v))


def forward_kernel(
    kind, start, count, own, pulled, grouped, tiles, first, weight, cot,
    out, gpre, wterm, buf, sup, sems,
):
    nb, slots, blk = tiles.shape[0], tiles.shape[1], tiles.shape[2]

    def issue(s, _):
        row = pl.multiple_of(start[s], blk)
        dst, sem = buf.at[pl.ds(pl.multiple_of(s * blk, blk), blk)], sems.at[s]
        for code, src in enumerate((own, pulled, grouped)):

            @pl.when(kind[s] == code)
            def _(src=src):
                pltpu.make_async_copy(src.at[pl.ds(row, blk)], dst, sem).start()

        return 0

    lax.fori_loop(0, nb * slots, issue, 0)
    for i in range(nb):
        rows = pl.ds(i * blk, blk)
        live = count[i]
        mix = jnp.concatenate(
            [
                jnp.where(t < live, tiles[i, t], jnp.zeros_like(tiles[i, t]))
                for t in range(slots)
            ],
            axis=1,
        )

        def land(t, _):
            s = i * slots + t
            dst = buf.at[pl.ds(pl.multiple_of(s * blk, blk), blk)]
            pltpu.make_async_copy(own.at[pl.ds(0, blk)], dst, sems.at[s]).wait()
            return 0

        lax.fori_loop(0, slots, land, 0)
        acc = jnp.dot(
            mix, buf[pl.ds(i * slots * blk, slots * blk)], preferred_element_type=jnp.float32
        )
        s16 = (
            (1.0 - alpha_mix) * acc + alpha_mix * first[rows].astype(jnp.float32)
        ).astype(jnp.bfloat16)
        sup[rows] = s16
        mixed = jnp.dot(s16, weight[...], preferred_element_type=jnp.float32)
        pre = (1.0 - beta_map) * s16.astype(jnp.float32) + beta_map * mixed
        sg = sigmoid(pre)
        out[rows] = (pre * sg).astype(jnp.bfloat16)
        gpre[rows] = (
            cot[rows].astype(jnp.float32) * sg * (1.0 + pre * (1.0 - sg))
        ).astype(jnp.bfloat16)
    wterm[...] = lax.dot_general(
        sup[...], gpre[...], (((0,), (0,)), ((), ())), preferred_element_type=jnp.float32
    ).astype(jnp.bfloat16)


def backward_kernel(cols, count, tiles, gpre, weight, glayer, gsup, acc):
    nb, slots, blk = tiles.shape[0], tiles.shape[1], tiles.shape[2]
    gp = gpre[...]
    back = lax.dot_general(
        gp, weight[...], (((1,), (1,)), ((), ())), preferred_element_type=jnp.float32
    )
    gsup[...] = ((1.0 - beta_map) * gp.astype(jnp.float32) + beta_map * back).astype(
        jnp.bfloat16
    ).reshape(gsup.shape)
    acc[...] = jnp.zeros_like(acc)

    def spread(s, _):
        i = s // slots
        col = cols[s]

        @pl.when((s - i * slots < count[i]) & (col >= 0) & (col < nb))
        def _():
            acc[col] += lax.dot_general(
                tiles[i, s - i * slots],
                gsup[i],
                (((0,), (0,)), ((), ())),
                preferred_element_type=jnp.float32,
            )

        return 0

    lax.fori_loop(0, nb * slots, spread, 0)
    glayer[...] = ((1.0 - alpha_mix) * acc[...]).astype(jnp.bfloat16).reshape(glayer.shape)


VM = pl.BlockSpec(memory_space=pltpu.VMEM)
SM = pl.BlockSpec(memory_space=pltpu.SMEM)
HB = pl.BlockSpec(memory_space=pl.ANY)


def per_device(
    layer_in, first_layer, weight, tiles, tile_cols, tile_count, history,
    member_serve, group_serve, push_pick, push_row, cotangent,
):
    nb, slots = tile_cols.shape
    feat = layer_in.shape[1]
    blk = tiles.shape[2]
    members = member_serve.shape[1]
    groups = group_serve.shape[1]
    rows = layer_in.shape[0]
    hb = history.shape[0] // blk
    stored = history.reshape(hb, blk, feat)

    pulled = lax.all_gather(history, MEMBER, axis=0, tiled=True)
    served = exchange(member_serve.reshape(members, 1), MEMBER)[:, 0]
    grouped = exchange(stored[group_serve[0]], GROUP).reshape(-1, feat)

    cols = tile_cols.reshape(-1)
    c = jnp.clip(cols, 0, nb + members + groups - 1)
    p = jnp.clip(c - nb, 0, members - 1)
    kind = (c >= nb).astype(jnp.int32) + (c >= nb + members).astype(jnp.int32)
    start = blk * jnp.where(
        kind == 0, c, jnp.where(kind == 1, p * hb + served[p], c - nb - members)
    )

    full = jax.ShapeDtypeStruct((rows, feat), jnp.bfloat16)
    square = jax.ShapeDtypeStruct((feat, feat), jnp.bfloat16)
    layer_out, grad_pre, wterm = pl.pallas_call(
        forward_kernel,
        name="pull_forward",
        out_shape=(full, full, square),
        in_specs=[SM, SM, SM, HB, HB, HB, VM, VM, VM, VM],
        out_specs=(VM, VM, VM),
        scratch_shapes=[
            pltpu.VMEM((nb * slots * blk, feat), jnp.bfloat16),
            pltpu.VMEM((rows, feat), jnp.bfloat16),
            pltpu.SemaphoreType.DMA((nb * slots,)),
        ],
    )(kind, start, tile_count, layer_in, pulled, grouped, tiles, first_layer, weight, cotangent)

    plane = lax.axis_size(PLANE)
    depth = lax.axis_size("z")
    w1 = exchange(wterm.reshape(plane, feat // plane, feat), PLANE)
    outgoing = layer_out[push_pick.reshape(members, -1)]
    arrived = exchange(outgoing, MEMBER)

    grad_layer = pl.pallas_call(
        backward_kernel,
        name="spread_backward",
        out_shape=full,
        in_specs=[SM, SM, VM, VM, VM],
        out_specs=VM,
        scratch_shapes=[
            pltpu.VMEM((nb, blk, feat), jnp.bfloat16),
            pltpu.VMEM((nb, blk, feat), jnp.float32),
        ],
    )(cols, tile_count, tiles, grad_pre, weight)

    s1 = jnp.sum(w1.astype(jnp.float32), axis=0).astype(jnp.bfloat16)
    w2 = exchange(jnp.broadcast_to(s1[None], (depth,) + s1.shape), "z")
    s2 = (beta_map * jnp.sum(w2.astype(jnp.float32), axis=0)).astype(jnp.bfloat16)
    w3 = exchange(jnp.broadcast_to(s2[None], (plane,) + s2.shape), PLANE)
    grad_weight = w3.reshape(feat, feat)

    new_history = history.at[push_row.reshape(-1)].set(
        arrived.reshape(-1, feat), unique_indices=True
    )
    return layer_out, grad_layer, grad_weight, new_history


def solution(mesh):
    fine = Mesh(mesh.devices.reshape(4, 4, 16, 2), ALL)
    r2, r3 = P(ALL, None), P(ALL, None, None)
    in_specs = (r2, r2, P(), P(ALL, None, None, None), r2, P(ALL), r2, r2, r2, r3, r3, r2)
    out_specs = (r2, r2, P(), r2)
    return jax.shard_map(
        per_device, mesh=fine, in_specs=in_specs, out_specs=out_specs, check_vma=False
    )
```

```python
import math

import jax
import jax.numpy as jnp
from jax import lax
from jax.experimental import pallas as pl
from jax.experimental.pallas import tpu as pltpu
from jax.sharding import Mesh, PartitionSpec as P

alpha_mix = 0.1
beta_map = math.log(1.5)

PLANE = ("y", "x", "core")
MEMBER = ("z", "core")
GROUP = ("y", "x")
ALL = ("y", "x", "z", "core")


def exchange(x, axes):
    return lax.all_to_all(x, axes, split_axis=0, concat_axis=0, tiled=True)


def sigmoid(v):
    return 1.0 / (1.0 + jnp.exp(-v))


def forward_kernel(
    kind, start, count, own, pulled, grouped, tiles, first, weight, cot,
    out, gpre, wterm, buf, sup, sems,
):
    nb, slots, blk = tiles.shape[0], tiles.shape[1], tiles.shape[2]

    def issue(s, _):
        row = pl.multiple_of(start[s], blk)
        dst, sem = buf.at[pl.ds(pl.multiple_of(s * blk, blk), blk)], sems.at[s]
        for code, src in enumerate((own, pulled, grouped)):

            @pl.when(kind[s] == code)
            def _(src=src):
                pltpu.make_async_copy(src.at[pl.ds(row, blk)], dst, sem).start()

        return 0

    lax.fori_loop(0, nb * slots, issue, 0)
    for i in range(nb):
        rows = pl.ds(i * blk, blk)
        live = count[i]
        mix = jnp.concatenate(
            [
                jnp.where(t < live, tiles[i, t], jnp.zeros_like(tiles[i, t]))
                for t in range(slots)
            ],
            axis=1,
        )

        def land(t, _):
            s = i * slots + t
            dst = buf.at[pl.ds(pl.multiple_of(s * blk, blk), blk)]
            pltpu.make_async_copy(own.at[pl.ds(0, blk)], dst, sems.at[s]).wait()
            return 0

        lax.fori_loop(0, slots, land, 0)
        acc = jnp.dot(
            mix, buf[pl.ds(i * slots * blk, slots * blk)], preferred_element_type=jnp.float32
        )
        s16 = (
            (1.0 - alpha_mix) * acc + alpha_mix * first[rows].astype(jnp.float32)
        ).astype(jnp.bfloat16)
        sup[rows] = s16
        mixed = jnp.dot(s16, weight[...], preferred_element_type=jnp.float32)
        pre = (1.0 - beta_map) * s16.astype(jnp.float32) + beta_map * mixed
        sg = sigmoid(pre)
        out[rows] = (pre * sg).astype(jnp.bfloat16)
        gpre[rows] = (
            cot[rows].astype(jnp.float32) * sg * (1.0 + pre * (1.0 - sg))
        ).astype(jnp.bfloat16)
    wterm[...] = lax.dot_general(
        sup[...], gpre[...], (((0,), (0,)), ((), ())), preferred_element_type=jnp.float32
    ).astype(jnp.bfloat16)


def backward_kernel(cols, count, tiles, gpre, weight, glayer, gsup, acc):
    nb, slots, blk = tiles.shape[0], tiles.shape[1], tiles.shape[2]
    gp = gpre[...]
    back = lax.dot_general(
        gp, weight[...], (((1,), (1,)), ((), ())), preferred_element_type=jnp.float32
    )
    gsup[...] = ((1.0 - beta_map) * gp.astype(jnp.float32) + beta_map * back).astype(
        jnp.bfloat16
    ).reshape(gsup.shape)
    acc[...] = jnp.zeros_like(acc)

    def spread(s, _):
        i = s // slots
        col = cols[s]

        @pl.when((s - i * slots < count[i]) & (col >= 0) & (col < nb))
        def _():
            acc[col] += lax.dot_general(
                tiles[i, s - i * slots],
                gsup[i],
                (((0,), (0,)), ((), ())),
                preferred_element_type=jnp.float32,
            )

        return 0

    lax.fori_loop(0, nb * slots, spread, 0)
    glayer[...] = ((1.0 - alpha_mix) * acc[...]).astype(jnp.bfloat16).reshape(glayer.shape)


def pick_kernel(pick, rows, keep, pass_on):
    n, m = pick.shape[0], rows.shape[0]
    hot = (lax.broadcasted_iota(jnp.int32, (n, m), 1) == pick[...]).astype(jnp.bfloat16)
    chosen = jnp.dot(hot, rows[...], preferred_element_type=jnp.float32).astype(jnp.bfloat16)
    keep[...] = chosen[: n // 2]
    pass_on[...] = chosen[n // 2 :]


def pack_kernel(parts, keep, passed, packed):
    terms, mine, feat = parts.shape
    depth = packed.shape[0]
    each = keep.shape[0] // depth
    total = parts[0].astype(jnp.float32)
    for k in range(1, terms):
        total += parts[k].astype(jnp.float32)
    packed[:, :mine] = jnp.broadcast_to(total.astype(jnp.bfloat16)[None], (depth, mine, feat))
    packed[:, mine : mine + each] = keep[...].reshape(depth, each, feat)
    packed[:, mine + each :] = passed[...].reshape(depth, each, feat)


def finish_kernel(parts, spread):
    depth, mine = parts.shape[0], spread.shape[1]
    total = parts[0, :mine].astype(jnp.float32)
    for k in range(1, depth):
        total += parts[k, :mine].astype(jnp.float32)
    spread[...] = jnp.broadcast_to((beta_map * total).astype(jnp.bfloat16)[None], spread.shape)


def push_kernel(target, packed, history, updated):
    n = history.shape[0]
    depth, tall, feat = packed.shape
    each = target.shape[1] // depth
    arrived = packed[:, tall - each :].reshape(depth * each, feat)
    hit = lax.broadcasted_iota(jnp.int32, (n, depth * each), 0) == target[...]
    moved = jnp.dot(
        hit.astype(jnp.bfloat16), arrived, preferred_element_type=jnp.float32
    ).astype(jnp.bfloat16)
    named = jnp.max(hit.astype(jnp.float32), axis=1, keepdims=True) > 0.0
    updated[...] = jnp.where(named, moved, history[...])


VM = pl.BlockSpec(memory_space=pltpu.VMEM)
SM = pl.BlockSpec(memory_space=pltpu.SMEM)
HB = pl.BlockSpec(memory_space=pl.ANY)


def per_device(
    layer_in, first_layer, weight, tiles, tile_cols, tile_count, history,
    member_serve, group_serve, push_pick, push_row, cotangent,
):
    nb, slots = tile_cols.shape
    feat = layer_in.shape[1]
    blk = tiles.shape[2]
    members = member_serve.shape[1]
    groups = group_serve.shape[1]
    rows = layer_in.shape[0]
    hb = history.shape[0] // blk
    stored = history.reshape(hb, blk, feat)

    pulled = lax.all_gather(history, MEMBER, axis=0, tiled=True)
    served = exchange(member_serve.reshape(members, 1), MEMBER)[:, 0]
    grouped = exchange(stored[group_serve[0]], GROUP).reshape(-1, feat)

    cols = tile_cols.reshape(-1)
    c = jnp.clip(cols, 0, nb + members + groups - 1)
    p = jnp.clip(c - nb, 0, members - 1)
    kind = (c >= nb).astype(jnp.int32) + (c >= nb + members).astype(jnp.int32)
    start = blk * jnp.where(
        kind == 0, c, jnp.where(kind == 1, p * hb + served[p], c - nb - members)
    )

    full = jax.ShapeDtypeStruct((rows, feat), jnp.bfloat16)
    square = jax.ShapeDtypeStruct((feat, feat), jnp.bfloat16)
    layer_out, grad_pre, wterm = pl.pallas_call(
        forward_kernel,
        name="pull_forward",
        out_shape=(full, full, square),
        in_specs=[SM, SM, SM, HB, HB, HB, VM, VM, VM, VM],
        out_specs=(VM, VM, VM),
        scratch_shapes=[
            pltpu.VMEM((nb * slots * blk, feat), jnp.bfloat16),
            pltpu.VMEM((rows, feat), jnp.bfloat16),
            pltpu.SemaphoreType.DMA((nb * slots,)),
        ],
    )(kind, start, tile_count, layer_in, pulled, grouped, tiles, first_layer, weight, cotangent)

    plane = lax.axis_size(PLANE)
    depth = lax.axis_size("z")
    mine = feat // plane
    core = lax.axis_index("core")
    per = push_pick.shape[2]
    picks = push_pick.reshape(depth, 2, per).transpose(1, 0, 2)
    picks = jnp.where(core == 0, picks, picks[::-1]).reshape(-1, 1)
    targets = push_row.reshape(depth, 2, per)
    targets = jnp.where(core == 0, targets, targets[:, ::-1]).reshape(1, -1)

    w1 = exchange(wterm.reshape(plane, mine, feat), PLANE)
    half = jax.ShapeDtypeStruct((depth * per, feat), jnp.bfloat16)
    keep, pass_on = pl.pallas_call(
        pick_kernel,
        name="push_pick",
        out_shape=(half, half),
        in_specs=[VM, VM],
        out_specs=(VM, VM),
    )(picks, layer_out)
    passed = lax.ppermute(pass_on, "core", [(0, 1), (1, 0)])
    grad_layer = pl.pallas_call(
        backward_kernel,
        name="spread_backward",
        out_shape=full,
        in_specs=[SM, SM, VM, VM, VM],
        out_specs=VM,
        scratch_shapes=[
            pltpu.VMEM((nb, blk, feat), jnp.bfloat16),
            pltpu.VMEM((nb, blk, feat), jnp.float32),
        ],
    )(cols, tile_count, tiles, grad_pre, weight)

    packed = pl.pallas_call(
        pack_kernel,
        name="pack",
        out_shape=jax.ShapeDtypeStruct((depth, mine + 2 * per, feat), jnp.bfloat16),
        in_specs=[VM, VM, VM],
        out_specs=VM,
    )(w1, keep, passed)
    w2 = exchange(packed, "z")
    w3 = exchange(
        pl.pallas_call(
            finish_kernel,
            name="finish",
            out_shape=jax.ShapeDtypeStruct((plane, mine, feat), jnp.bfloat16),
            in_specs=[VM],
            out_specs=VM,
        )(w2),
        PLANE,
    )
    grad_weight = w3.reshape(feat, feat)

    new_history = pl.pallas_call(
        push_kernel,
        name="push_store",
        out_shape=jax.ShapeDtypeStruct(history.shape, jnp.bfloat16),
        in_specs=[VM, VM, VM],
        out_specs=VM,
    )(targets, w2, history)
    return layer_out, grad_layer, grad_weight, new_history


def solution(mesh):
    fine = Mesh(mesh.devices.reshape(4, 4, 16, 2), ALL)
    r2, r3 = P(ALL, None), P(ALL, None, None)
    in_specs = (r2, r2, P(), P(ALL, None, None, None), r2, P(ALL), r2, r2, r2, r3, r3, r2)
    out_specs = (r2, r2, P(), r2)
    return jax.shard_map(
        per_device, mesh=fine, in_specs=in_specs, out_specs=out_specs, check_vma=False
    )
```

```python
import math

import jax
import jax.numpy as jnp
from jax import lax
from jax.experimental import pallas as pl
from jax.experimental.pallas import tpu as pltpu
from jax.sharding import Mesh, PartitionSpec as P

alpha_mix = 0.1
beta_map = math.log(1.5)

PLANE = ("y", "x", "core")
MEMBER = ("z", "core")
GROUP = ("y", "x")
ALL = ("y", "x", "z", "core")
MEMBERS = 32


def exchange(x, axes):
    return lax.all_to_all(x, axes, split_axis=0, concat_axis=0, tiled=True)


def sigmoid(v):
    return 1.0 / (1.0 + jnp.exp(-v))


def local_kernel(cols, count, own, grouped, tiles, first, base, mix):
    nb, slots, blk = tiles.shape[0], tiles.shape[1], tiles.shape[2]
    offset = nb + MEMBERS
    base[...] = alpha_mix * first[...].astype(jnp.float32)
    mix[...] = jnp.zeros_like(mix)

    def add(i, t, src, row):
        rows = pl.ds(pl.multiple_of(i * blk, blk), blk)
        base[rows] += (1.0 - alpha_mix) * jnp.dot(
            tiles[i, t],
            src[pl.ds(pl.multiple_of(row, blk), blk)],
            preferred_element_type=jnp.float32,
        )

    def slot(s, _):
        i = s // slots
        t = s - i * slots
        col = cols[s]
        live = t < count[i]

        @pl.when(live & (col < nb))
        def _():
            add(i, t, own, col * blk)

        @pl.when(live & (col >= offset))
        def _():
            add(i, t, grouped, (col - offset) * blk)

        @pl.when(live & (col >= nb) & (col < offset))
        def _():
            mix[i, t] = tiles[i, t]

        return 0

    lax.fori_loop(0, nb * slots, slot, 0)


def forward_kernel(
    take, start, pulled, mix_in, base_in, weight_in, cot_in, out, gpre, wterm,
    buf, mix, base, weight, cot, acts, grads, sup, term, slot_sems, sems,
):
    nb, slots, blk = mix.shape[0], mix.shape[1], mix.shape[2]
    feat = weight.shape[0]

    def fetch(s):
        row = pl.multiple_of(start[s], blk)
        dst = buf.at[pl.ds(pl.multiple_of(s * blk, blk), blk)]
        return pltpu.make_async_copy(pulled.at[pl.ds(row, blk)], dst, slot_sems.at[s])

    def issue(s, _):
        @pl.when(take[s] == 1)
        def _():
            fetch(s).start()

        @pl.when(take[s] != 1)
        def _():
            buf[pl.ds(pl.multiple_of(s * blk, blk), blk)] = jnp.zeros(
                (blk, feat), jnp.bfloat16
            )

        return 0

    def rows(i):
        return pl.ds(i * blk, blk)

    def mix_copy(i):
        return pltpu.make_async_copy(mix_in.at[i], mix.at[i], sems.at[i])

    def base_copy(i):
        return pltpu.make_async_copy(base_in.at[rows(i)], base.at[rows(i)], sems.at[nb + i])

    def out_copy(i):
        return pltpu.make_async_copy(acts.at[rows(i)], out.at[rows(i)], sems.at[2 * nb + i])

    def grad_copy(i):
        return pltpu.make_async_copy(grads.at[rows(i)], gpre.at[rows(i)], sems.at[3 * nb + i])

    weight_copy = pltpu.make_async_copy(weight_in, weight, sems.at[4 * nb])
    cot_copy = pltpu.make_async_copy(cot_in, cot, sems.at[4 * nb + 1])
    term_copy = pltpu.make_async_copy(term, wterm, sems.at[4 * nb + 2])

    for i in range(nb):
        lax.fori_loop(i * slots, (i + 1) * slots, issue, 0)
        mix_copy(i).start()
        base_copy(i).start()
        if i == 0:
            weight_copy.start()
            cot_copy.start()
    for i in range(nb):

        def land(s, _):
            @pl.when(take[s] == 1)
            def _():
                fetch(s).wait()

            return 0

        lax.fori_loop(i * slots, (i + 1) * slots, land, 0)
        mix_copy(i).wait()
        base_copy(i).wait()
        acc = jnp.dot(
            jnp.concatenate([mix[i, t] for t in range(slots)], axis=1),
            buf[pl.ds(i * slots * blk, slots * blk)],
            preferred_element_type=jnp.float32,
        )
        s16 = ((1.0 - alpha_mix) * acc + base[rows(i)]).astype(jnp.bfloat16)
        sup[rows(i)] = s16
        if i == 0:
            weight_copy.wait()
            cot_copy.wait()
        mixed = jnp.dot(s16, weight[...], preferred_element_type=jnp.float32)
        pre = (1.0 - beta_map) * s16.astype(jnp.float32) + beta_map * mixed
        sg = sigmoid(pre)
        acts[rows(i)] = (pre * sg).astype(jnp.bfloat16)
        grads[rows(i)] = (
            cot[rows(i)].astype(jnp.float32) * sg * (1.0 + pre * (1.0 - sg))
        ).astype(jnp.bfloat16)
        out_copy(i).start()
        grad_copy(i).start()
    term[...] = lax.dot_general(
        sup[...], grads[...], (((0,), (0,)), ((), ())), preferred_element_type=jnp.float32
    ).astype(jnp.bfloat16)
    term_copy.start()
    for i in range(nb):
        out_copy(i).wait()
        grad_copy(i).wait()
    term_copy.wait()


def backward_kernel(cols, count, tiles, gpre, weight, glayer, gsup, acc):
    nb, slots, blk = tiles.shape[0], tiles.shape[1], tiles.shape[2]
    gp = gpre[...]
    back = lax.dot_general(
        gp, weight[...], (((1,), (1,)), ((), ())), preferred_element_type=jnp.float32
    )
    gsup[...] = ((1.0 - beta_map) * gp.astype(jnp.float32) + beta_map * back).astype(
        jnp.bfloat16
    ).reshape(gsup.shape)
    acc[...] = jnp.zeros_like(acc)

    def spread(s, _):
        i = s // slots
        col = cols[s]

        @pl.when((s - i * slots < count[i]) & (col >= 0) & (col < nb))
        def _():
            acc[col] += lax.dot_general(
                tiles[i, s - i * slots],
                gsup[i],
                (((0,), (0,)), ((), ())),
                preferred_element_type=jnp.float32,
            )

        return 0

    lax.fori_loop(0, nb * slots, spread, 0)
    glayer[...] = ((1.0 - alpha_mix) * acc[...]).astype(jnp.bfloat16).reshape(glayer.shape)


def pick_kernel(pick, rows, keep, pass_on):
    n, m = pick.shape[0], rows.shape[0]
    hot = (lax.broadcasted_iota(jnp.int32, (n, m), 1) == pick[...]).astype(jnp.bfloat16)
    chosen = jnp.dot(hot, rows[...], preferred_element_type=jnp.float32).astype(jnp.bfloat16)
    keep[...] = chosen[: n // 2]
    pass_on[...] = chosen[n // 2 :]


def pack_kernel(parts, keep, passed, packed):
    terms, mine, feat = parts.shape
    depth = packed.shape[0]
    each = keep.shape[0] // depth
    total = parts[0].astype(jnp.float32)
    for k in range(1, terms):
        total += parts[k].astype(jnp.float32)
    packed[:, :mine] = jnp.broadcast_to(total.astype(jnp.bfloat16)[None], (depth, mine, feat))
    packed[:, mine : mine + each] = keep[...].reshape(depth, each, feat)
    packed[:, mine + each :] = passed[...].reshape(depth, each, feat)


def finish_kernel(parts, spread):
    depth, mine = parts.shape[0], spread.shape[1]
    total = parts[0, :mine].astype(jnp.float32)
    for k in range(1, depth):
        total += parts[k, :mine].astype(jnp.float32)
    spread[...] = jnp.broadcast_to((beta_map * total).astype(jnp.bfloat16)[None], spread.shape)


def push_kernel(target, packed, history, updated):
    n = history.shape[0]
    depth, tall, feat = packed.shape
    each = target.shape[1] // depth
    arrived = packed[:, tall - each :].reshape(depth * each, feat)
    hit = lax.broadcasted_iota(jnp.int32, (n, depth * each), 0) == target[...]
    moved = jnp.dot(
        hit.astype(jnp.bfloat16), arrived, preferred_element_type=jnp.float32
    ).astype(jnp.bfloat16)
    named = jnp.max(hit.astype(jnp.float32), axis=1, keepdims=True) > 0.0
    updated[...] = jnp.where(named, moved, history[...])


VM = pl.BlockSpec(memory_space=pltpu.VMEM)
SM = pl.BlockSpec(memory_space=pltpu.SMEM)
HB = pl.BlockSpec(memory_space=pltpu.HBM)


def near(x):
    return pltpu.with_memory_space_constraint(x, pltpu.VMEM)


def far(x):
    return pltpu.with_memory_space_constraint(x, pltpu.HBM)


def call(kernel, name, outs, in_specs, scratch=(), out_spec=VM):
    return pl.pallas_call(
        kernel,
        name=name,
        out_shape=outs,
        in_specs=in_specs,
        out_specs=jax.tree.map(lambda _: out_spec, outs),
        scratch_shapes=list(scratch),
        compiler_params=pltpu.CompilerParams(vmem_limit_bytes=24 * 2**20),
    )


def per_device(
    layer_in, first_layer, weight, tiles, tile_cols, tile_count, history,
    member_serve, group_serve, push_pick, push_row, cotangent,
):
    nb, slots = tile_cols.shape
    feat = layer_in.shape[1]
    blk = tiles.shape[2]
    members = member_serve.shape[1]
    groups = group_serve.shape[1]
    rows = layer_in.shape[0]
    hb = history.shape[0] // blk
    stored = history.reshape(hb, blk, feat)

    pulled = lax.all_gather(history, MEMBER, axis=0, tiled=True)
    served = exchange(member_serve.reshape(members, 1), MEMBER)[:, 0]
    grouped = exchange(stored[group_serve[0]], GROUP).reshape(-1, feat)

    cols = tile_cols.reshape(-1)
    live = (jnp.arange(slots) < tile_count[:, None]).reshape(-1)
    take = (live & (cols >= nb) & (cols < nb + members)).astype(jnp.int32)
    p = jnp.clip(cols - nb, 0, members - 1)
    start = blk * (p * hb + served[p])

    base, mix = call(
        local_kernel,
        "local_sum",
        (
            jax.ShapeDtypeStruct((rows, feat), jnp.float32),
            jax.ShapeDtypeStruct(tiles.shape, jnp.bfloat16),
        ),
        [SM, SM, VM, VM, VM, VM],
    )(cols, tile_count, layer_in, near(grouped), tiles, first_layer)
    full = jax.ShapeDtypeStruct((rows, feat), jnp.bfloat16)
    block = pltpu.VMEM((rows, feat), jnp.bfloat16)
    far_full = pltpu.HBM((rows, feat), jnp.bfloat16)
    layer_out, grad_pre, wterm = call(
        forward_kernel,
        "pull_forward",
        (far_full, far_full, pltpu.HBM((feat, feat), jnp.bfloat16)),
        [SM, SM, HB, HB, HB, HB, HB],
        [
            pltpu.VMEM((nb * slots * blk, feat), jnp.bfloat16),
            pltpu.VMEM(tiles.shape, jnp.bfloat16),
            pltpu.VMEM((rows, feat), jnp.float32),
            pltpu.VMEM((feat, feat), jnp.bfloat16),
            block,
            block,
            block,
            block,
            pltpu.VMEM((feat, feat), jnp.bfloat16),
            pltpu.SemaphoreType.DMA((nb * slots,)),
            pltpu.SemaphoreType.DMA((4 * nb + 3,)),
        ],
        HB,
    )(take, start, far(pulled), far(mix), far(base), far(weight), far(cotangent))

    plane = lax.axis_size(PLANE)
    depth = lax.axis_size("z")
    mine = feat // plane
    core = lax.axis_index("core")
    per = push_pick.shape[2]
    picks = push_pick.reshape(depth, 2, per).transpose(1, 0, 2)
    picks = jnp.where(core == 0, picks, picks[::-1]).reshape(-1, 1)
    targets = push_row.reshape(depth, 2, per)
    targets = jnp.where(core == 0, targets, targets[:, ::-1]).reshape(1, -1)

    w1 = exchange(wterm.reshape(plane, mine, feat), PLANE)
    half = jax.ShapeDtypeStruct((depth * per, feat), jnp.bfloat16)
    keep, pass_on = call(pick_kernel, "push_pick", (half, half), [VM, VM])(
        picks, layer_out
    )
    passed = lax.ppermute(pass_on, "core", [(0, 1), (1, 0)])
    grad_layer = call(
        backward_kernel,
        "spread_backward",
        full,
        [SM, SM, VM, VM, VM],
        [
            pltpu.VMEM((nb, blk, feat), jnp.bfloat16),
            pltpu.VMEM((nb, blk, feat), jnp.float32),
        ],
    )(cols, tile_count, tiles, grad_pre, weight)

    packed = call(
        pack_kernel,
        "pack",
        jax.ShapeDtypeStruct((depth, mine + 2 * per, feat), jnp.bfloat16),
        [VM, VM, VM],
    )(near(w1), near(keep), near(passed))
    w2 = near(exchange(packed, "z"))
    share = jax.ShapeDtypeStruct((plane, mine, feat), jnp.bfloat16)
    w3 = exchange(call(finish_kernel, "finish", share, [VM])(w2), PLANE)
    grad_weight = w3.reshape(feat, feat)

    new_history = call(
        push_kernel, "push_store", jax.ShapeDtypeStruct(history.shape, jnp.bfloat16), [VM, VM, VM]
    )(targets, w2, history)
    return layer_out, grad_layer, grad_weight, new_history


def solution(mesh):
    fine = Mesh(mesh.devices.reshape(4, 4, 16, 2), ALL)
    r2, r3 = P(ALL, None), P(ALL, None, None)
    in_specs = (r2, r2, P(), P(ALL, None, None, None), r2, P(ALL), r2, r2, r2, r3, r3, r2)
    out_specs = (r2, r2, P(), r2)
    return jax.shard_map(
        per_device, mesh=fine, in_specs=in_specs, out_specs=out_specs, check_vma=False
    )
```

```python
import math

import jax
import jax.numpy as jnp
from jax import lax
from jax.experimental import pallas as pl
from jax.experimental.pallas import tpu as pltpu
from jax.sharding import Mesh, PartitionSpec as P

alpha_mix = 0.1
beta_map = math.log(1.5)

GROUP = ("y", "x")
PLANE = ("y", "x", "core")
DEPTH = ("zh", "zl")
MEMBER = ("zh", "zl", "core")
SHARE = ("y", "x", "core", "zl")
ALL = ("y", "x", "zh", "zl", "core")
MEMBERS = 32


def exchange(x, axes):
    return lax.all_to_all(x, axes, split_axis=0, concat_axis=0, tiled=True)


def sigmoid(v):
    return 1.0 / (1.0 + jnp.exp(-v))


def local_kernel(cols, count, own, grouped, tiles, first, base, mix):
    nb, slots, blk = tiles.shape[0], tiles.shape[1], tiles.shape[2]
    offset = nb + MEMBERS
    base[...] = alpha_mix * first[...].astype(jnp.float32)
    mix[...] = jnp.zeros_like(mix)

    def add(i, t, src, row):
        rows = pl.ds(pl.multiple_of(i * blk, blk), blk)
        base[rows] += (1.0 - alpha_mix) * jnp.dot(
            tiles[i, t],
            src[pl.ds(pl.multiple_of(row, blk), blk)],
            preferred_element_type=jnp.float32,
        )

    def slot(s, _):
        i = s // slots
        t = s - i * slots
        col = cols[s]
        live = t < count[i]

        @pl.when(live & (col < nb))
        def _():
            add(i, t, own, col * blk)

        @pl.when(live & (col >= offset))
        def _():
            add(i, t, grouped, (col - offset) * blk)

        @pl.when(live & (col >= nb) & (col < offset))
        def _():
            mix[i, t] = tiles[i, t]

        return 0

    lax.fori_loop(0, nb * slots, slot, 0)


def forward_kernel(
    take, start, pulled, mix_in, base_in, weight_in, cot_in, out, gpre, wterm,
    buf, mix, base, weight, cot, acts, grads, sup, term, slot_sems, sems,
):
    nb, slots, blk = mix.shape[0], mix.shape[1], mix.shape[2]
    feat = weight.shape[0]

    def fetch(s):
        row = pl.multiple_of(start[s], blk)
        dst = buf.at[pl.ds(pl.multiple_of(s * blk, blk), blk)]
        return pltpu.make_async_copy(pulled.at[pl.ds(row, blk)], dst, slot_sems.at[s])

    def issue(s, _):
        @pl.when(take[s] == 1)
        def _():
            fetch(s).start()

        @pl.when(take[s] != 1)
        def _():
            buf[pl.ds(pl.multiple_of(s * blk, blk), blk)] = jnp.zeros(
                (blk, feat), jnp.bfloat16
            )

        return 0

    def rows(i):
        return pl.ds(i * blk, blk)

    def mix_copy(i):
        return pltpu.make_async_copy(mix_in.at[i], mix.at[i], sems.at[i])

    def base_copy(i):
        return pltpu.make_async_copy(base_in.at[rows(i)], base.at[rows(i)], sems.at[nb + i])

    def out_copy(i):
        return pltpu.make_async_copy(acts.at[rows(i)], out.at[rows(i)], sems.at[2 * nb + i])

    def grad_copy(i):
        return pltpu.make_async_copy(grads.at[rows(i)], gpre.at[rows(i)], sems.at[3 * nb + i])

    weight_copy = pltpu.make_async_copy(weight_in, weight, sems.at[4 * nb])
    cot_copy = pltpu.make_async_copy(cot_in, cot, sems.at[4 * nb + 1])
    term_copy = pltpu.make_async_copy(term, wterm, sems.at[4 * nb + 2])

    for i in range(nb):
        lax.fori_loop(i * slots, (i + 1) * slots, issue, 0)
        mix_copy(i).start()
        base_copy(i).start()
        if i == 0:
            weight_copy.start()
            cot_copy.start()
    for i in range(nb):

        def land(s, _):
            @pl.when(take[s] == 1)
            def _():
                fetch(s).wait()

            return 0

        lax.fori_loop(i * slots, (i + 1) * slots, land, 0)
        mix_copy(i).wait()
        base_copy(i).wait()
        acc = jnp.dot(
            jnp.concatenate([mix[i, t] for t in range(slots)], axis=1),
            buf[pl.ds(i * slots * blk, slots * blk)],
            preferred_element_type=jnp.float32,
        )
        s16 = ((1.0 - alpha_mix) * acc + base[rows(i)]).astype(jnp.bfloat16)
        sup[rows(i)] = s16
        if i == 0:
            weight_copy.wait()
            cot_copy.wait()
        mixed = jnp.dot(s16, weight[...], preferred_element_type=jnp.float32)
        pre = (1.0 - beta_map) * s16.astype(jnp.float32) + beta_map * mixed
        sg = sigmoid(pre)
        acts[rows(i)] = (pre * sg).astype(jnp.bfloat16)
        grads[rows(i)] = (
            cot[rows(i)].astype(jnp.float32) * sg * (1.0 + pre * (1.0 - sg))
        ).astype(jnp.bfloat16)
        out_copy(i).start()
        grad_copy(i).start()
    term[...] = lax.dot_general(
        sup[...], grads[...], (((0,), (0,)), ((), ())), preferred_element_type=jnp.float32
    ).astype(jnp.bfloat16)
    term_copy.start()
    for i in range(nb):
        out_copy(i).wait()
        grad_copy(i).wait()
    term_copy.wait()


def backward_kernel(cols, count, tiles, gpre, weight, glayer, gsup, acc):
    nb, slots, blk = tiles.shape[0], tiles.shape[1], tiles.shape[2]
    gp = gpre[...]
    back = lax.dot_general(
        gp, weight[...], (((1,), (1,)), ((), ())), preferred_element_type=jnp.float32
    )
    gsup[...] = ((1.0 - beta_map) * gp.astype(jnp.float32) + beta_map * back).astype(
        jnp.bfloat16
    ).reshape(gsup.shape)
    acc[...] = jnp.zeros_like(acc)

    def spread(s, _):
        i = s // slots
        col = cols[s]

        @pl.when((s - i * slots < count[i]) & (col >= 0) & (col < nb))
        def _():
            acc[col] += lax.dot_general(
                tiles[i, s - i * slots],
                gsup[i],
                (((0,), (0,)), ((), ())),
                preferred_element_type=jnp.float32,
            )

        return 0

    lax.fori_loop(0, nb * slots, spread, 0)
    glayer[...] = ((1.0 - alpha_mix) * acc[...]).astype(jnp.bfloat16).reshape(glayer.shape)


def pick_kernel(pick, rows, keep, pass_on):
    n, m = pick.shape[0], rows.shape[0]
    hot = (lax.broadcasted_iota(jnp.int32, (n, m), 1) == pick[...]).astype(jnp.bfloat16)
    chosen = jnp.dot(hot, rows[...], preferred_element_type=jnp.float32).astype(jnp.bfloat16)
    keep[...] = chosen[: n // 2]
    pass_on[...] = chosen[n // 2 :]


def pack_kernel(parts, keep, passed, packed):
    terms, mine, feat = parts.shape
    depth, tall = packed.shape[0], packed.shape[1]
    each = keep.shape[0] // depth
    share = tall - 2 * each
    cuts = mine // share
    total = parts[0].astype(jnp.float32)
    for k in range(1, terms):
        total += parts[k].astype(jnp.float32)
    pieces = [total[c * share : (c + 1) * share].astype(jnp.bfloat16) for c in range(cuts)]
    for z in range(depth):
        packed[z, :share] = pieces[z % cuts]
    packed[:, share : share + each] = keep[...].reshape(depth, each, feat)
    packed[:, share + each :] = passed[...].reshape(depth, each, feat)


def finish_kernel(parts, spread):
    depth, share = parts.shape[0], spread.shape[1]
    total = parts[0, :share].astype(jnp.float32)
    for k in range(1, depth):
        total += parts[k, :share].astype(jnp.float32)
    spread[...] = jnp.broadcast_to((beta_map * total).astype(jnp.bfloat16)[None], spread.shape)


def push_kernel(target, packed, history, updated):
    n = history.shape[0]
    depth, tall, feat = packed.shape
    each = target.shape[1] // depth
    arrived = packed[:, tall - each :].reshape(depth * each, feat)
    hit = lax.broadcasted_iota(jnp.int32, (n, depth * each), 0) == target[...]
    moved = jnp.dot(
        hit.astype(jnp.bfloat16), arrived, preferred_element_type=jnp.float32
    ).astype(jnp.bfloat16)
    named = jnp.max(hit.astype(jnp.float32), axis=1, keepdims=True) > 0.0
    updated[...] = jnp.where(named, moved, history[...])


VM = pl.BlockSpec(memory_space=pltpu.VMEM)
SM = pl.BlockSpec(memory_space=pltpu.SMEM)
HB = pl.BlockSpec(memory_space=pltpu.HBM)


def near(x):
    return pltpu.with_memory_space_constraint(x, pltpu.VMEM)


def far(x):
    return pltpu.with_memory_space_constraint(x, pltpu.HBM)


def call(kernel, name, outs, in_specs, scratch=(), out_spec=VM):
    return pl.pallas_call(
        kernel,
        name=name,
        out_shape=outs,
        in_specs=in_specs,
        out_specs=jax.tree.map(lambda _: out_spec, outs),
        scratch_shapes=list(scratch),
        compiler_params=pltpu.CompilerParams(vmem_limit_bytes=24 * 2**20),
    )


def per_device(
    layer_in, first_layer, weight, tiles, tile_cols, tile_count, history,
    member_serve, group_serve, push_pick, push_row, cotangent,
):
    nb, slots = tile_cols.shape
    feat = layer_in.shape[1]
    blk = tiles.shape[2]
    members = member_serve.shape[1]
    groups = group_serve.shape[1]
    rows = layer_in.shape[0]
    hb = history.shape[0] // blk
    stored = history.reshape(hb, blk, feat)

    pulled = lax.all_gather(history, MEMBER, axis=0, tiled=True)
    served = exchange(member_serve.reshape(members, 1), MEMBER)[:, 0]
    grouped = exchange(stored[group_serve[0]], GROUP).reshape(-1, feat)

    cols = tile_cols.reshape(-1)
    live = (jnp.arange(slots) < tile_count[:, None]).reshape(-1)
    take = (live & (cols >= nb) & (cols < nb + members)).astype(jnp.int32)
    p = jnp.clip(cols - nb, 0, members - 1)
    start = blk * (p * hb + served[p])

    base, mix = call(
        local_kernel,
        "local_sum",
        (
            jax.ShapeDtypeStruct((rows, feat), jnp.float32),
            jax.ShapeDtypeStruct(tiles.shape, jnp.bfloat16),
        ),
        [SM, SM, VM, VM, VM, VM],
    )(cols, tile_count, layer_in, near(grouped), tiles, first_layer)
    full = jax.ShapeDtypeStruct((rows, feat), jnp.bfloat16)
    block = pltpu.VMEM((rows, feat), jnp.bfloat16)
    far_full = pltpu.HBM((rows, feat), jnp.bfloat16)
    layer_out, grad_pre, wterm = call(
        forward_kernel,
        "pull_forward",
        (far_full, far_full, pltpu.HBM((feat, feat), jnp.bfloat16)),
        [SM, SM, HB, HB, HB, HB, HB],
        [
            pltpu.VMEM((nb * slots * blk, feat), jnp.bfloat16),
            pltpu.VMEM(tiles.shape, jnp.bfloat16),
            pltpu.VMEM((rows, feat), jnp.float32),
            pltpu.VMEM((feat, feat), jnp.bfloat16),
            block,
            block,
            block,
            block,
            pltpu.VMEM((feat, feat), jnp.bfloat16),
            pltpu.SemaphoreType.DMA((nb * slots,)),
            pltpu.SemaphoreType.DMA((4 * nb + 3,)),
        ],
        HB,
    )(take, start, far(pulled), far(mix), far(base), far(weight), far(cotangent))

    plane = lax.axis_size(PLANE)
    depth = lax.axis_size(DEPTH)
    mine = feat // plane
    sharers = lax.axis_size(SHARE)
    share = feat // sharers
    core = lax.axis_index("core")
    per = push_pick.shape[2]
    picks = push_pick.reshape(depth, 2, per).transpose(1, 0, 2)
    picks = jnp.where(core == 0, picks, picks[::-1]).reshape(-1, 1)
    targets = push_row.reshape(depth, 2, per)
    targets = jnp.where(core == 0, targets, targets[:, ::-1]).reshape(1, -1)

    w1 = exchange(wterm.reshape(plane, mine, feat), PLANE)
    half = jax.ShapeDtypeStruct((depth * per, feat), jnp.bfloat16)
    keep, pass_on = call(pick_kernel, "push_pick", (half, half), [VM, VM])(
        picks, layer_out
    )
    passed = lax.ppermute(pass_on, "core", [(0, 1), (1, 0)])
    grad_layer = call(
        backward_kernel,
        "spread_backward",
        full,
        [SM, SM, VM, VM, VM],
        [
            pltpu.VMEM((nb, blk, feat), jnp.bfloat16),
            pltpu.VMEM((nb, blk, feat), jnp.float32),
        ],
    )(cols, tile_count, tiles, grad_pre, weight)

    packed = call(
        pack_kernel,
        "pack",
        jax.ShapeDtypeStruct((depth, share + 2 * per, feat), jnp.bfloat16),
        [VM, VM, VM],
    )(near(w1), near(keep), near(passed))
    w2 = near(exchange(packed, DEPTH))
    shared = jax.ShapeDtypeStruct((sharers, share, feat), jnp.bfloat16)
    w3 = exchange(call(finish_kernel, "finish", shared, [VM])(w2), SHARE)
    grad_weight = w3.reshape(feat, feat)

    new_history = call(
        push_kernel, "push_store", jax.ShapeDtypeStruct(history.shape, jnp.bfloat16), [VM, VM, VM]
    )(targets, w2, history)
    return layer_out, grad_layer, grad_weight, new_history


def solution(mesh):
    fine = Mesh(mesh.devices.reshape(4, 4, 8, 2, 2), ALL)
    r2, r3 = P(ALL, None), P(ALL, None, None)
    in_specs = (r2, r2, P(), P(ALL, None, None, None), r2, P(ALL), r2, r2, r2, r3, r3, r2)
    out_specs = (r2, r2, P(), r2)
    return jax.shard_map(
        per_device, mesh=fine, in_specs=in_specs, out_specs=out_specs, check_vma=False
    )
```

```python
import math

import jax
import jax.numpy as jnp
from jax import lax
from jax.experimental import pallas as pl
from jax.experimental.pallas import tpu as pltpu
from jax.sharding import Mesh, PartitionSpec as P

alpha_mix = 0.1
beta_map = math.log(1.5)

GROUP = ("y", "x")
PLANE = ("y", "x", "core")
DEPTH = ("zh", "zl")
MEMBER = ("zh", "zl", "core")
SHARE = ("y", "x", "core", "zl")
ALL = ("y", "x", "zh", "zl", "core")
MEMBERS = 32
HELD = 2


def exchange(x, axes):
    return lax.all_to_all(x, axes, split_axis=0, concat_axis=0, tiled=True)


def sigmoid(v):
    return 1.0 / (1.0 + jnp.exp(-v))


def local_kernel(
    cols, count, served, own, grouped, tiles, first, base, mix, start, found
):
    nb, slots, blk = tiles.shape[0], tiles.shape[1], tiles.shape[2]
    offset = nb + MEMBERS
    base[...] = alpha_mix * first[...].astype(jnp.float32)
    mix[...] = jnp.zeros_like(mix)

    def add(i, t, src, row):
        rows = pl.ds(pl.multiple_of(i * blk, blk), blk)
        base[rows] += (1.0 - alpha_mix) * jnp.dot(
            tiles[i, t],
            src[pl.ds(pl.multiple_of(row, blk), blk)],
            preferred_element_type=jnp.float32,
        )

    def block_row(i, _):
        def slot(t, n):
            col = cols[i * slots + t]
            live = t < count[i]
            far_off = live & (col >= nb) & (col < offset)

            @pl.when(live & (col >= 0) & (col < nb))
            def _():
                add(i, t, own, col * blk)

            @pl.when(live & (col >= offset))
            def _():
                add(i, t, grouped, (col - offset) * blk)

            @pl.when(far_off)
            def _():
                mix[i, n] = tiles[i, t]
                start[i * slots + n] = blk * ((col - nb) * HELD + served[col - nb])

            return n + far_off.astype(jnp.int32)

        found[i] = lax.fori_loop(0, slots, slot, jnp.int32(0))
        return 0

    lax.fori_loop(0, nb, block_row, 0)


def forward_kernel(
    found, start, pulled, mix_in, base_in, weight_in, cot_in, out, gpre, wterm,
    buf, acc, mix, base, weight, cot, acts, grads, sup, term, slot_sems, sems,
):
    nb, slots, blk = mix.shape[0], mix.shape[1], mix.shape[2]
    feat = weight.shape[0]

    def fetch(s):
        row = pl.multiple_of(start[s], blk)
        return pltpu.make_async_copy(pulled.at[pl.ds(row, blk)], buf.at[s], slot_sems.at[s])

    def rows(i):
        return pl.ds(i * blk, blk)

    def mix_copy(i):
        return pltpu.make_async_copy(mix_in.at[i], mix.at[i], sems.at[i])

    def base_copy(i):
        return pltpu.make_async_copy(base_in.at[rows(i)], base.at[rows(i)], sems.at[nb + i])

    def out_copy(i):
        return pltpu.make_async_copy(acts.at[rows(i)], out.at[rows(i)], sems.at[2 * nb + i])

    def grad_copy(i):
        return pltpu.make_async_copy(grads.at[rows(i)], gpre.at[rows(i)], sems.at[3 * nb + i])

    weight_copy = pltpu.make_async_copy(weight_in, weight, sems.at[4 * nb])
    cot_copy = pltpu.make_async_copy(cot_in, cot, sems.at[4 * nb + 1])
    term_copy = pltpu.make_async_copy(term, wterm, sems.at[4 * nb + 2])

    for i in range(nb):
        n = found[i]

        def issue(t, _, i=i):
            fetch(i * slots + t).start()
            return 0

        lax.fori_loop(0, n, issue, 0)

        @pl.when(n == 0)
        def _(i=i):
            buf[i * slots] = jnp.zeros((blk, feat), jnp.bfloat16)
            buf[i * slots + 1] = jnp.zeros((blk, feat), jnp.bfloat16)

        @pl.when(lax.rem(n, 2) == 1)
        def _(i=i, n=n):
            buf[i * slots + n] = jnp.zeros((blk, feat), jnp.bfloat16)

        mix_copy(i).start()
        base_copy(i).start()
        if i == 0:
            weight_copy.start()
            cot_copy.start()
    for i in range(nb):
        n = found[i]

        def land(t, _, i=i):
            fetch(i * slots + t).wait()
            return 0

        lax.fori_loop(0, n, land, 0)
        mix_copy(i).wait()
        base_copy(i).wait()

        def pair(j, i=i):
            both = jnp.concatenate([mix[i, 2 * j], mix[i, 2 * j + 1]], axis=1)
            src = buf[pl.ds(i * slots + 2 * j, 2)].reshape(2 * blk, feat)
            return jnp.dot(both, src, preferred_element_type=jnp.float32)

        def more(j, _):
            acc[...] += pair(j)
            return 0

        acc[...] = pair(0)
        lax.fori_loop(1, (n + 1) // 2, more, 0)
        s16 = ((1.0 - alpha_mix) * acc[...] + base[rows(i)]).astype(jnp.bfloat16)
        sup[rows(i)] = s16
        if i == 0:
            weight_copy.wait()
            cot_copy.wait()
        mixed = jnp.dot(s16, weight[...], preferred_element_type=jnp.float32)
        pre = (1.0 - beta_map) * s16.astype(jnp.float32) + beta_map * mixed
        sg = sigmoid(pre)
        acts[rows(i)] = (pre * sg).astype(jnp.bfloat16)
        grads[rows(i)] = (
            cot[rows(i)].astype(jnp.float32) * sg * (1.0 + pre * (1.0 - sg))
        ).astype(jnp.bfloat16)
        out_copy(i).start()
        grad_copy(i).start()
    term[...] = lax.dot_general(
        sup[...], grads[...], (((0,), (0,)), ((), ())), preferred_element_type=jnp.float32
    ).astype(jnp.bfloat16)
    term_copy.start()
    for i in range(nb):
        out_copy(i).wait()
        grad_copy(i).wait()
    term_copy.wait()


def backward_kernel(cols, count, tiles, gpre, weight, glayer, gsup, acc):
    nb, slots, blk = tiles.shape[0], tiles.shape[1], tiles.shape[2]
    gp = gpre[...]
    back = lax.dot_general(
        gp, weight[...], (((1,), (1,)), ((), ())), preferred_element_type=jnp.float32
    )
    gsup[...] = ((1.0 - beta_map) * gp.astype(jnp.float32) + beta_map * back).astype(
        jnp.bfloat16
    ).reshape(gsup.shape)
    acc[...] = jnp.zeros_like(acc)

    def spread(s, _):
        i = s // slots
        col = cols[s]

        @pl.when((s - i * slots < count[i]) & (col >= 0) & (col < nb))
        def _():
            acc[col] += lax.dot_general(
                tiles[i, s - i * slots],
                gsup[i],
                (((0,), (0,)), ((), ())),
                preferred_element_type=jnp.float32,
            )

        return 0

    lax.fori_loop(0, nb * slots, spread, 0)
    glayer[...] = ((1.0 - alpha_mix) * acc[...]).astype(jnp.bfloat16).reshape(glayer.shape)


def pick_kernel(pick, rows, keep, pass_on):
    n, m = pick.shape[0], rows.shape[0]
    hot = (lax.broadcasted_iota(jnp.int32, (n, m), 1) == pick[...]).astype(jnp.bfloat16)
    chosen = jnp.dot(hot, rows[...], preferred_element_type=jnp.float32).astype(jnp.bfloat16)
    keep[...] = chosen[: n // 2]
    pass_on[...] = chosen[n // 2 :]


def pack_kernel(parts, keep, passed, packed):
    terms, mine, feat = parts.shape
    depth, tall = packed.shape[0], packed.shape[1]
    each = keep.shape[0] // depth
    share = tall - 2 * each
    cuts = mine // share
    total = parts[0].astype(jnp.float32)
    for k in range(1, terms):
        total += parts[k].astype(jnp.float32)
    pieces = [total[c * share : (c + 1) * share].astype(jnp.bfloat16) for c in range(cuts)]
    for z in range(depth):
        packed[z, :share] = pieces[z % cuts]
    packed[:, share : share + each] = keep[...].reshape(depth, each, feat)
    packed[:, share + each :] = passed[...].reshape(depth, each, feat)


def finish_kernel(parts, spread):
    depth, share = parts.shape[0], spread.shape[1]
    total = parts[0, :share].astype(jnp.float32)
    for k in range(1, depth):
        total += parts[k, :share].astype(jnp.float32)
    spread[...] = jnp.broadcast_to((beta_map * total).astype(jnp.bfloat16)[None], spread.shape)


def push_kernel(target, packed, history, updated):
    n = history.shape[0]
    depth, tall, feat = packed.shape
    each = target.shape[1] // depth
    arrived = packed[:, tall - each :].reshape(depth * each, feat)
    hit = lax.broadcasted_iota(jnp.int32, (n, depth * each), 0) == target[...]
    moved = jnp.dot(
        hit.astype(jnp.bfloat16), arrived, preferred_element_type=jnp.float32
    ).astype(jnp.bfloat16)
    named = jnp.max(hit.astype(jnp.float32), axis=1, keepdims=True) > 0.0
    updated[...] = jnp.where(named, moved, history[...])


VM = pl.BlockSpec(memory_space=pltpu.VMEM)
SM = pl.BlockSpec(memory_space=pltpu.SMEM)
HB = pl.BlockSpec(memory_space=pltpu.HBM)


def near(x):
    return pltpu.with_memory_space_constraint(x, pltpu.VMEM)


def far(x):
    return pltpu.with_memory_space_constraint(x, pltpu.HBM)


def call(kernel, name, outs, in_specs, scratch=(), out_specs=None):
    return pl.pallas_call(
        kernel,
        name=name,
        out_shape=outs,
        in_specs=in_specs,
        out_specs=out_specs or jax.tree.map(lambda _: VM, outs),
        scratch_shapes=list(scratch),
        compiler_params=pltpu.CompilerParams(vmem_limit_bytes=24 * 2**20),
    )


def per_device(
    layer_in, first_layer, weight, tiles, tile_cols, tile_count, history,
    member_serve, group_serve, push_pick, push_row, cotangent,
):
    nb, slots = tile_cols.shape
    feat = layer_in.shape[1]
    blk = tiles.shape[2]
    members = member_serve.shape[1]
    groups = group_serve.shape[1]
    rows = layer_in.shape[0]
    hb = history.shape[0] // blk
    stored = history.reshape(hb, blk, feat)

    pulled = lax.all_gather(history, MEMBER, axis=0, tiled=True)
    served = exchange(member_serve.reshape(members, 1), MEMBER)[:, 0]
    grouped = exchange(stored[group_serve[0]], GROUP).reshape(-1, feat)

    cols = tile_cols.reshape(-1)
    base, mix, start, found = call(
        local_kernel,
        "local_sum",
        (
            jax.ShapeDtypeStruct((rows, feat), jnp.float32),
            jax.ShapeDtypeStruct(tiles.shape, jnp.bfloat16),
            jax.ShapeDtypeStruct((nb * slots,), jnp.int32),
            jax.ShapeDtypeStruct((nb,), jnp.int32),
        ),
        [SM, SM, SM, VM, VM, VM, VM],
        out_specs=(VM, VM, SM, SM),
    )(cols, tile_count, served, layer_in, near(grouped), tiles, first_layer)
    full = jax.ShapeDtypeStruct((rows, feat), jnp.bfloat16)
    block = pltpu.VMEM((rows, feat), jnp.bfloat16)
    far_full = pltpu.HBM((rows, feat), jnp.bfloat16)
    layer_out, grad_pre, wterm = call(
        forward_kernel,
        "pull_forward",
        (far_full, far_full, pltpu.HBM((feat, feat), jnp.bfloat16)),
        [SM, SM, HB, HB, HB, HB, HB],
        [
            pltpu.VMEM((nb * slots, blk, feat), jnp.bfloat16),
            pltpu.VMEM((blk, feat), jnp.float32),
            pltpu.VMEM(tiles.shape, jnp.bfloat16),
            pltpu.VMEM((rows, feat), jnp.float32),
            pltpu.VMEM((feat, feat), jnp.bfloat16),
            block,
            block,
            block,
            block,
            pltpu.VMEM((feat, feat), jnp.bfloat16),
            pltpu.SemaphoreType.DMA((nb * slots,)),
            pltpu.SemaphoreType.DMA((4 * nb + 3,)),
        ],
        (HB, HB, HB),
    )(found, start, far(pulled), far(mix), far(base), far(weight), far(cotangent))

    plane = lax.axis_size(PLANE)
    depth = lax.axis_size(DEPTH)
    mine = feat // plane
    sharers = lax.axis_size(SHARE)
    share = feat // sharers
    core = lax.axis_index("core")
    per = push_pick.shape[2]
    picks = push_pick.reshape(depth, 2, per).transpose(1, 0, 2)
    picks = jnp.where(core == 0, picks, picks[::-1]).reshape(-1, 1)
    targets = push_row.reshape(depth, 2, per)
    targets = jnp.where(core == 0, targets, targets[:, ::-1]).reshape(1, -1)

    w1 = exchange(wterm.reshape(plane, mine, feat), PLANE)
    half = jax.ShapeDtypeStruct((depth * per, feat), jnp.bfloat16)
    keep, pass_on = call(pick_kernel, "push_pick", (half, half), [VM, VM])(
        picks, layer_out
    )
    passed = lax.ppermute(pass_on, "core", [(0, 1), (1, 0)])
    grad_layer = call(
        backward_kernel,
        "spread_backward",
        full,
        [SM, SM, VM, VM, VM],
        [
            pltpu.VMEM((nb, blk, feat), jnp.bfloat16),
            pltpu.VMEM((nb, blk, feat), jnp.float32),
        ],
    )(cols, tile_count, tiles, grad_pre, weight)

    packed = call(
        pack_kernel,
        "pack",
        jax.ShapeDtypeStruct((depth, share + 2 * per, feat), jnp.bfloat16),
        [VM, VM, VM],
    )(near(w1), near(keep), near(passed))
    w2 = near(exchange(packed, DEPTH))
    shared = jax.ShapeDtypeStruct((sharers, share, feat), jnp.bfloat16)
    w3 = exchange(call(finish_kernel, "finish", shared, [VM])(w2), SHARE)
    grad_weight = w3.reshape(feat, feat)

    new_history = call(
        push_kernel, "push_store", jax.ShapeDtypeStruct(history.shape, jnp.bfloat16), [VM, VM, VM]
    )(targets, w2, history)
    return layer_out, grad_layer, grad_weight, new_history


def solution(mesh):
    fine = Mesh(mesh.devices.reshape(4, 4, 8, 2, 2), ALL)
    r2, r3 = P(ALL, None), P(ALL, None, None)
    in_specs = (r2, r2, P(), P(ALL, None, None, None), r2, P(ALL), r2, r2, r2, r3, r3, r2)
    out_specs = (r2, r2, P(), r2)
    return jax.shard_map(
        per_device, mesh=fine, in_specs=in_specs, out_specs=out_specs, check_vma=False
    )
```

```python
import math

import jax
import jax.numpy as jnp
from jax import lax
from jax.experimental import pallas as pl
from jax.experimental.pallas import tpu as pltpu
from jax.sharding import Mesh, PartitionSpec as P

alpha_mix = 0.1
beta_map = math.log(1.5)

GROUP = ("y", "x")
PLANE = ("y", "x", "core")
DEPTH = ("zh", "zl")
MEMBER = ("zh", "zl", "core")
SHARE = ("y", "x", "core", "zl")
ALL = ("y", "x", "zh", "zl", "core")
MEMBERS = 32


def exchange(x, axes):
    return lax.all_to_all(x, axes, split_axis=0, concat_axis=0, tiled=True)


def sigmoid(v):
    return lax.logistic(v)


def local_kernel(cols, count, own, grouped, tiles, first, base, mix):
    nb, slots, blk = tiles.shape[0], tiles.shape[1], tiles.shape[2]
    offset = nb + MEMBERS
    base[...] = alpha_mix * first[...].astype(jnp.float32)
    mix[...] = jnp.zeros_like(mix)

    def add(i, t, src, row):
        rows = pl.ds(pl.multiple_of(i * blk, blk), blk)
        base[rows] += (1.0 - alpha_mix) * jnp.dot(
            tiles[i, t],
            src[pl.ds(pl.multiple_of(row, blk), blk)],
            preferred_element_type=jnp.float32,
        )

    def slot(s, _):
        i = s // slots
        t = s - i * slots
        col = cols[s]
        live = t < count[i]

        @pl.when(live & (col < nb))
        def _():
            add(i, t, own, col * blk)

        @pl.when(live & (col >= offset))
        def _():
            add(i, t, grouped, (col - offset) * blk)

        @pl.when(live & (col >= nb) & (col < offset))
        def _():
            mix[i, t] = tiles[i, t]

        return 0

    lax.fori_loop(0, nb * slots, slot, 0)


def forward_kernel(
    take, start, pulled, mix_in, base_in, weight_in, cot_in, out, gpre, wterm,
    buf, mix, base, weight, cot, acts, grads, sup, term, slot_sems, sems,
):
    nb, slots, blk = mix.shape[0], mix.shape[1], mix.shape[2]
    feat = weight.shape[0]

    def fetch(s):
        row = pl.multiple_of(start[s], blk)
        dst = buf.at[pl.ds(pl.multiple_of(s * blk, blk), blk)]
        return pltpu.make_async_copy(pulled.at[pl.ds(row, blk)], dst, slot_sems.at[s])

    def issue(s):
        @pl.when(take[s] == 1)
        def _():
            fetch(s).start()

        @pl.when(take[s] != 1)
        def _():
            buf[pl.ds(pl.multiple_of(s * blk, blk), blk)] = jnp.zeros(
                (blk, feat), jnp.bfloat16
            )

    def rows(i):
        return pl.ds(i * blk, blk)

    def mix_copy(i):
        return pltpu.make_async_copy(mix_in.at[i], mix.at[i], sems.at[i])

    def base_copy(i):
        return pltpu.make_async_copy(base_in.at[rows(i)], base.at[rows(i)], sems.at[nb + i])

    def out_copy(i):
        return pltpu.make_async_copy(acts.at[rows(i)], out.at[rows(i)], sems.at[2 * nb + i])

    def grad_copy(i):
        return pltpu.make_async_copy(grads.at[rows(i)], gpre.at[rows(i)], sems.at[3 * nb + i])

    weight_copy = pltpu.make_async_copy(weight_in, weight, sems.at[4 * nb])
    cot_copy = pltpu.make_async_copy(cot_in, cot, sems.at[4 * nb + 1])
    term_copy = pltpu.make_async_copy(term, wterm, sems.at[4 * nb + 2])

    for i in range(nb):
        for s in range(i * slots, (i + 1) * slots):
            issue(s)
        mix_copy(i).start()
        base_copy(i).start()
        if i == 0:
            weight_copy.start()
            cot_copy.start()
    for i in range(nb):

        def land(s):
            @pl.when(take[s] == 1)
            def _():
                fetch(s).wait()

        for s in range(i * slots, (i + 1) * slots):
            land(s)
        mix_copy(i).wait()
        base_copy(i).wait()
        acc = jnp.dot(
            jnp.concatenate([mix[i, t] for t in range(slots)], axis=1),
            buf[pl.ds(i * slots * blk, slots * blk)],
            preferred_element_type=jnp.float32,
        )
        s16 = ((1.0 - alpha_mix) * acc + base[rows(i)]).astype(jnp.bfloat16)
        sup[rows(i)] = s16
        if i == 0:
            weight_copy.wait()
            cot_copy.wait()
        mixed = jnp.dot(s16, weight[...], preferred_element_type=jnp.float32)
        pre = (1.0 - beta_map) * s16.astype(jnp.float32) + beta_map * mixed
        sg = sigmoid(pre)
        acts[rows(i)] = (pre * sg).astype(jnp.bfloat16)
        grads[rows(i)] = (
            cot[rows(i)].astype(jnp.float32) * sg * (1.0 + pre * (1.0 - sg))
        ).astype(jnp.bfloat16)
        out_copy(i).start()
        grad_copy(i).start()
    term[...] = lax.dot_general(
        sup[...], grads[...], (((0,), (0,)), ((), ())), preferred_element_type=jnp.float32
    ).astype(jnp.bfloat16)
    term_copy.start()
    for i in range(nb):
        out_copy(i).wait()
        grad_copy(i).wait()
    term_copy.wait()


def backward_kernel(cols, count, tiles, gpre, weight, glayer, gsup, acc):
    nb, slots, blk = tiles.shape[0], tiles.shape[1], tiles.shape[2]
    gp = gpre[...]
    back = lax.dot_general(
        gp, weight[...], (((1,), (1,)), ((), ())), preferred_element_type=jnp.float32
    )
    gsup[...] = ((1.0 - beta_map) * gp.astype(jnp.float32) + beta_map * back).astype(
        jnp.bfloat16
    ).reshape(gsup.shape)
    acc[...] = jnp.zeros_like(acc)

    def spread(s, _):
        i = s // slots
        col = cols[s]

        @pl.when((s - i * slots < count[i]) & (col >= 0) & (col < nb))
        def _():
            acc[col] += lax.dot_general(
                tiles[i, s - i * slots],
                gsup[i],
                (((0,), (0,)), ((), ())),
                preferred_element_type=jnp.float32,
            )

        return 0

    lax.fori_loop(0, nb * slots, spread, 0)
    glayer[...] = ((1.0 - alpha_mix) * acc[...]).astype(jnp.bfloat16).reshape(glayer.shape)


def pick_kernel(pick, rows, keep, pass_on):
    n, m = pick.shape[0], rows.shape[0]
    hot = (lax.broadcasted_iota(jnp.int32, (n, m), 1) == pick[...]).astype(jnp.bfloat16)
    chosen = jnp.dot(hot, rows[...], preferred_element_type=jnp.float32).astype(jnp.bfloat16)
    keep[...] = chosen[: n // 2]
    pass_on[...] = chosen[n // 2 :]


def pack_kernel(parts, keep, passed, packed):
    terms, mine, feat = parts.shape
    depth, tall = packed.shape[0], packed.shape[1]
    each = keep.shape[0] // depth
    share = tall - 2 * each
    cuts = mine // share
    total = parts[0].astype(jnp.float32)
    for k in range(1, terms):
        total += parts[k].astype(jnp.float32)
    pieces = [total[c * share : (c + 1) * share].astype(jnp.bfloat16) for c in range(cuts)]
    for z in range(depth):
        packed[z, :share] = pieces[z % cuts]
    packed[:, share : share + each] = keep[...].reshape(depth, each, feat)
    packed[:, share + each :] = passed[...].reshape(depth, each, feat)


def finish_kernel(parts, spread):
    depth, share = parts.shape[0], parts.shape[1] // 2
    total = parts[0, :share].astype(jnp.float32)
    for k in range(1, depth):
        total += parts[k, :share].astype(jnp.float32)
    mine = (beta_map * total).astype(jnp.bfloat16)
    spread[...] = jnp.concatenate([mine] * (spread.shape[0] // share), axis=0)


def push_kernel(target, packed, history, updated):
    n = history.shape[0]
    depth, tall, feat = packed.shape
    each = target.shape[1] // depth
    arrived = packed[:, tall - each :].reshape(depth * each, feat)
    hit = lax.broadcasted_iota(jnp.int32, (n, depth * each), 0) == target[...]
    moved = jnp.dot(
        hit.astype(jnp.bfloat16), arrived, preferred_element_type=jnp.float32
    ).astype(jnp.bfloat16)
    named = jnp.max(hit.astype(jnp.float32), axis=1, keepdims=True) > 0.0
    updated[...] = jnp.where(named, moved, history[...])


VM = pl.BlockSpec(memory_space=pltpu.VMEM)
SM = pl.BlockSpec(memory_space=pltpu.SMEM)
HB = pl.BlockSpec(memory_space=pltpu.HBM)


def near(x):
    return pltpu.with_memory_space_constraint(x, pltpu.VMEM)


def far(x):
    return pltpu.with_memory_space_constraint(x, pltpu.HBM)


def call(kernel, name, outs, in_specs, scratch=(), out_spec=VM):
    return pl.pallas_call(
        kernel,
        name=name,
        out_shape=outs,
        in_specs=in_specs,
        out_specs=jax.tree.map(lambda _: out_spec, outs),
        scratch_shapes=list(scratch),
        compiler_params=pltpu.CompilerParams(vmem_limit_bytes=24 * 2**20),
    )


def per_device(
    layer_in, first_layer, weight, tiles, tile_cols, tile_count, history,
    member_serve, group_serve, push_pick, push_row, cotangent,
):
    nb, slots = tile_cols.shape
    feat = layer_in.shape[1]
    blk = tiles.shape[2]
    members = member_serve.shape[1]
    groups = group_serve.shape[1]
    rows = layer_in.shape[0]
    hb = history.shape[0] // blk
    stored = history.reshape(hb, blk, feat)

    pulled = lax.all_gather(history, MEMBER, axis=0, tiled=True)
    served = exchange(member_serve.reshape(members, 1), MEMBER)[:, 0]
    grouped = exchange(stored[group_serve[0]], GROUP).reshape(-1, feat)

    cols = tile_cols.reshape(-1)
    live = (jnp.arange(slots) < tile_count[:, None]).reshape(-1)
    take = (live & (cols >= nb) & (cols < nb + members)).astype(jnp.int32)
    p = jnp.clip(cols - nb, 0, members - 1)
    start = blk * (p * hb + served[p])

    base, mix = call(
        local_kernel,
        "local_sum",
        (
            jax.ShapeDtypeStruct((rows, feat), jnp.float32),
            jax.ShapeDtypeStruct(tiles.shape, jnp.bfloat16),
        ),
        [SM, SM, VM, VM, VM, VM],
    )(cols, tile_count, layer_in, near(grouped), tiles, first_layer)
    full = jax.ShapeDtypeStruct((rows, feat), jnp.bfloat16)
    block = pltpu.VMEM((rows, feat), jnp.bfloat16)
    far_full = pltpu.HBM((rows, feat), jnp.bfloat16)
    layer_out, grad_pre, wterm = call(
        forward_kernel,
        "pull_forward",
        (far_full, far_full, pltpu.HBM((feat, feat), jnp.bfloat16)),
        [SM, SM, HB, HB, HB, HB, HB],
        [
            pltpu.VMEM((nb * slots * blk, feat), jnp.bfloat16),
            pltpu.VMEM(tiles.shape, jnp.bfloat16),
            pltpu.VMEM((rows, feat), jnp.float32),
            pltpu.VMEM((feat, feat), jnp.bfloat16),
            block,
            block,
            block,
            block,
            pltpu.VMEM((feat, feat), jnp.bfloat16),
            pltpu.SemaphoreType.DMA((nb * slots,)),
            pltpu.SemaphoreType.DMA((4 * nb + 3,)),
        ],
        HB,
    )(take, start, far(pulled), far(mix), far(base), far(weight), far(cotangent))

    plane = lax.axis_size(PLANE)
    depth = lax.axis_size(DEPTH)
    mine = feat // plane
    sharers = lax.axis_size(SHARE)
    share = feat // sharers
    core = lax.axis_index("core")
    per = push_pick.shape[2]
    picks = push_pick.reshape(depth, 2, per).transpose(1, 0, 2)
    picks = jnp.where(core == 0, picks, picks[::-1]).reshape(-1, 1)
    targets = push_row.reshape(depth, 2, per)
    targets = jnp.where(core == 0, targets, targets[:, ::-1]).reshape(1, -1)

    w1 = exchange(wterm.reshape(plane, mine, feat), PLANE)
    half = jax.ShapeDtypeStruct((depth * per, feat), jnp.bfloat16)
    keep, pass_on = call(pick_kernel, "push_pick", (half, half), [VM, VM])(
        picks, layer_out
    )
    passed = lax.ppermute(pass_on, "core", [(0, 1), (1, 0)])
    grad_layer = call(
        backward_kernel,
        "spread_backward",
        full,
        [SM, SM, VM, VM, VM],
        [
            pltpu.VMEM((nb, blk, feat), jnp.bfloat16),
            pltpu.VMEM((nb, blk, feat), jnp.float32),
        ],
    )(cols, tile_count, tiles, grad_pre, weight)

    packed = call(
        pack_kernel,
        "pack",
        jax.ShapeDtypeStruct((depth, share + 2 * per, feat), jnp.bfloat16),
        [VM, VM, VM],
    )(near(w1), near(keep), near(passed))
    w2 = near(exchange(packed, DEPTH))
    square = jax.ShapeDtypeStruct((feat, feat), jnp.bfloat16)
    grad_weight = exchange(call(finish_kernel, "finish", square, [VM])(w2), SHARE)

    new_history = call(
        push_kernel, "push_store", jax.ShapeDtypeStruct(history.shape, jnp.bfloat16), [VM, VM, VM]
    )(targets, w2, history)
    return layer_out, grad_layer, grad_weight, new_history


def solution(mesh):
    fine = Mesh(mesh.devices.reshape(4, 4, 8, 2, 2), ALL)
    r2, r3 = P(ALL, None), P(ALL, None, None)
    in_specs = (r2, r2, P(), P(ALL, None, None, None), r2, P(ALL), r2, r2, r2, r3, r3, r2)
    out_specs = (r2, r2, P(), r2)
    return jax.shard_map(
        per_device, mesh=fine, in_specs=in_specs, out_specs=out_specs, check_vma=False
    )
```

```python
import math

import jax
import jax.numpy as jnp
from jax import lax
from jax.experimental import pallas as pl
from jax.experimental.pallas import tpu as pltpu
from jax.sharding import Mesh, PartitionSpec as P

alpha_mix = 0.1
beta_map = math.log(1.5)

GROUP = ("y", "x")
PLANE = ("y", "x", "core")
DEPTH = ("zh", "zl")
MEMBER = ("zh", "zl", "core")
SHARE = ("y", "x", "core", "zl")
ALL = ("y", "x", "zh", "zl", "core")
MEMBERS = 32


def exchange(x, axes):
    return lax.all_to_all(x, axes, split_axis=0, concat_axis=0, tiled=True)


def sigmoid(v):
    return lax.logistic(v)


def local_kernel(cols, count, own, grouped, tiles, first, base, mix):
    nb, slots, blk = tiles.shape[0], tiles.shape[1], tiles.shape[2]
    offset = nb + MEMBERS
    base[...] = alpha_mix * first[...].astype(jnp.float32)
    mix[...] = jnp.zeros_like(mix)

    def add(i, t, src, row):
        rows = pl.ds(pl.multiple_of(i * blk, blk), blk)
        base[rows] += (1.0 - alpha_mix) * jnp.dot(
            tiles[i, t],
            src[pl.ds(pl.multiple_of(row, blk), blk)],
            preferred_element_type=jnp.float32,
        )

    def slot(s, _):
        i = s // slots
        t = s - i * slots
        col = cols[s]
        live = t < count[i]

        @pl.when(live & (col < nb))
        def _():
            add(i, t, own, col * blk)

        @pl.when(live & (col >= offset))
        def _():
            add(i, t, grouped, (col - offset) * blk)

        @pl.when(live & (col >= nb) & (col < offset))
        def _():
            mix[i, t] = tiles[i, t]

        return 0

    lax.fori_loop(0, nb * slots, slot, 0)


def forward_kernel(
    take, start, pulled, mix_in, base_in, weight_in, cot_in, out, gpre, wterm,
    buf, mix, base, weight, cot, acts, grads, sup, term, slot_sems, sems,
):
    nb, slots, blk = mix.shape[0], mix.shape[1], mix.shape[2]
    feat = weight.shape[0]

    def fetch(s):
        row = pl.multiple_of(start[s], blk)
        dst = buf.at[pl.ds(pl.multiple_of(s * blk, blk), blk)]
        return pltpu.make_async_copy(pulled.at[pl.ds(row, blk)], dst, slot_sems.at[s])

    def issue(s):
        @pl.when(take[s] == 1)
        def _():
            fetch(s).start()

        @pl.when(take[s] != 1)
        def _():
            buf[pl.ds(pl.multiple_of(s * blk, blk), blk)] = jnp.zeros(
                (blk, feat), jnp.bfloat16
            )

    def rows(i):
        return pl.ds(i * blk, blk)

    def mix_copy(i):
        return pltpu.make_async_copy(mix_in.at[i], mix.at[i], sems.at[i])

    def base_copy(i):
        return pltpu.make_async_copy(base_in.at[rows(i)], base.at[rows(i)], sems.at[nb + i])

    def out_copy(i):
        return pltpu.make_async_copy(acts.at[rows(i)], out.at[rows(i)], sems.at[2 * nb + i])

    def grad_copy(i):
        return pltpu.make_async_copy(grads.at[rows(i)], gpre.at[rows(i)], sems.at[3 * nb + i])

    weight_copy = pltpu.make_async_copy(weight_in, weight, sems.at[4 * nb])
    cot_copy = pltpu.make_async_copy(cot_in, cot, sems.at[4 * nb + 1])
    term_copy = pltpu.make_async_copy(term, wterm, sems.at[4 * nb + 2])

    for i in range(nb):
        for s in range(i * slots, (i + 1) * slots):
            issue(s)
        mix_copy(i).start()
        base_copy(i).start()
        if i == 0:
            weight_copy.start()
            cot_copy.start()
    for i in range(nb):

        def land(s):
            @pl.when(take[s] == 1)
            def _():
                fetch(s).wait()

        for s in range(i * slots, (i + 1) * slots):
            land(s)
        mix_copy(i).wait()
        base_copy(i).wait()
        acc = jnp.dot(
            jnp.concatenate([mix[i, t] for t in range(slots)], axis=1),
            buf[pl.ds(i * slots * blk, slots * blk)],
            preferred_element_type=jnp.float32,
        )
        s16 = ((1.0 - alpha_mix) * acc + base[rows(i)]).astype(jnp.bfloat16)
        sup[rows(i)] = s16
        if i == 0:
            weight_copy.wait()
            cot_copy.wait()
        mixed = jnp.dot(s16, weight[...], preferred_element_type=jnp.float32)
        pre = (1.0 - beta_map) * s16.astype(jnp.float32) + beta_map * mixed
        sg = sigmoid(pre)
        acts[rows(i)] = (pre * sg).astype(jnp.bfloat16)
        grads[rows(i)] = (
            cot[rows(i)].astype(jnp.float32) * sg * (1.0 + pre * (1.0 - sg))
        ).astype(jnp.bfloat16)
        out_copy(i).start()
        grad_copy(i).start()
    term[...] = lax.dot_general(
        sup[...], grads[...], (((0,), (0,)), ((), ())), preferred_element_type=jnp.float32
    ).astype(jnp.bfloat16)
    term_copy.start()
    for i in range(nb):
        out_copy(i).wait()
        grad_copy(i).wait()
    term_copy.wait()


def backward_kernel(cols, count, tiles, gpre, weight, glayer, gsup, acc):
    nb, slots, blk = tiles.shape[0], tiles.shape[1], tiles.shape[2]
    gp = gpre[...]
    back = lax.dot_general(
        gp, weight[...], (((1,), (1,)), ((), ())), preferred_element_type=jnp.float32
    )
    gsup[...] = ((1.0 - beta_map) * gp.astype(jnp.float32) + beta_map * back).astype(
        jnp.bfloat16
    ).reshape(gsup.shape)
    acc[...] = jnp.zeros_like(acc)

    def spread(s, _):
        i = s // slots
        col = cols[s]

        @pl.when((s - i * slots < count[i]) & (col >= 0) & (col < nb))
        def _():
            acc[col] += lax.dot_general(
                tiles[i, s - i * slots],
                gsup[i],
                (((0,), (0,)), ((), ())),
                preferred_element_type=jnp.float32,
            )

        return 0

    lax.fori_loop(0, nb * slots, spread, 0)
    glayer[...] = ((1.0 - alpha_mix) * acc[...]).astype(jnp.bfloat16).reshape(glayer.shape)


def pick_kernel(pick, rows, keep, pass_on):
    n, m = pick.shape[0], rows.shape[0]
    hot = (lax.broadcasted_iota(jnp.int32, (n, m), 1) == pick[...]).astype(jnp.bfloat16)
    chosen = jnp.dot(hot, rows[...], preferred_element_type=jnp.float32).astype(jnp.bfloat16)
    keep[...] = chosen[: n // 2]
    pass_on[...] = chosen[n // 2 :]


def pack_kernel(parts, keep, passed, packed):
    terms, mine, feat = parts.shape
    depth, tall = packed.shape[0], packed.shape[1]
    each = keep.shape[0] // depth
    share = tall - 2 * each
    cuts = mine // share
    total = parts[0].astype(jnp.float32)
    for k in range(1, terms):
        total += parts[k].astype(jnp.float32)
    pieces = [total[c * share : (c + 1) * share].astype(jnp.bfloat16) for c in range(cuts)]
    for z in range(depth):
        packed[z, :share] = pieces[z % cuts]
    packed[:, share : share + each] = keep[...].reshape(depth, each, feat)
    packed[:, share + each :] = passed[...].reshape(depth, each, feat)


def finish_kernel(parts, spread):
    depth, share = parts.shape[0], parts.shape[1] // 2
    total = parts[0, :share].astype(jnp.float32)
    for k in range(1, depth):
        total += parts[k, :share].astype(jnp.float32)
    mine = (beta_map * total).astype(jnp.bfloat16)
    spread[...] = jnp.concatenate([mine] * (spread.shape[0] // share), axis=0)


def push_kernel(target, packed, passed, history, updated):
    n = history.shape[0]
    depth, tall, feat = packed.shape
    each = target.shape[1] // depth
    own = packed[:, tall - each : tall - each // 2]
    arrived = jnp.concatenate([own, passed[...]], axis=1).reshape(depth * each, feat)
    hit = lax.broadcasted_iota(jnp.int32, (n, depth * each), 0) == target[...]
    moved = jnp.dot(
        hit.astype(jnp.bfloat16), arrived, preferred_element_type=jnp.float32
    ).astype(jnp.bfloat16)
    named = jnp.max(hit.astype(jnp.float32), axis=1, keepdims=True) > 0.0
    updated[...] = jnp.where(named, moved, history[...])


VM = pl.BlockSpec(memory_space=pltpu.VMEM)
SM = pl.BlockSpec(memory_space=pltpu.SMEM)
HB = pl.BlockSpec(memory_space=pltpu.HBM)


def near(x):
    return pltpu.with_memory_space_constraint(x, pltpu.VMEM)


def far(x):
    return pltpu.with_memory_space_constraint(x, pltpu.HBM)


def call(kernel, name, outs, in_specs, scratch=(), out_spec=VM):
    return pl.pallas_call(
        kernel,
        name=name,
        out_shape=outs,
        in_specs=in_specs,
        out_specs=jax.tree.map(lambda _: out_spec, outs),
        scratch_shapes=list(scratch),
        compiler_params=pltpu.CompilerParams(vmem_limit_bytes=24 * 2**20),
    )


def per_device(
    layer_in, first_layer, weight, tiles, tile_cols, tile_count, history,
    member_serve, group_serve, push_pick, push_row, cotangent,
):
    nb, slots = tile_cols.shape
    feat = layer_in.shape[1]
    blk = tiles.shape[2]
    members = member_serve.shape[1]
    groups = group_serve.shape[1]
    rows = layer_in.shape[0]
    hb = history.shape[0] // blk
    stored = history.reshape(hb, blk, feat)

    pulled = lax.all_gather(history, MEMBER, axis=0, tiled=True)
    served = exchange(member_serve.reshape(members, 1), MEMBER)[:, 0]
    grouped = exchange(stored[group_serve[0]], GROUP).reshape(-1, feat)

    cols = tile_cols.reshape(-1)
    live = (jnp.arange(slots) < tile_count[:, None]).reshape(-1)
    take = (live & (cols >= nb) & (cols < nb + members)).astype(jnp.int32)
    p = jnp.clip(cols - nb, 0, members - 1)
    start = blk * (p * hb + served[p])

    base, mix = call(
        local_kernel,
        "local_sum",
        (
            jax.ShapeDtypeStruct((rows, feat), jnp.float32),
            jax.ShapeDtypeStruct(tiles.shape, jnp.bfloat16),
        ),
        [SM, SM, VM, VM, VM, VM],
    )(cols, tile_count, layer_in, near(grouped), tiles, first_layer)
    full = jax.ShapeDtypeStruct((rows, feat), jnp.bfloat16)
    block = pltpu.VMEM((rows, feat), jnp.bfloat16)
    far_full = pltpu.HBM((rows, feat), jnp.bfloat16)
    layer_out, grad_pre, wterm = call(
        forward_kernel,
        "pull_forward",
        (far_full, far_full, pltpu.HBM((feat, feat), jnp.bfloat16)),
        [SM, SM, HB, HB, HB, HB, HB],
        [
            pltpu.VMEM((nb * slots * blk, feat), jnp.bfloat16),
            pltpu.VMEM(tiles.shape, jnp.bfloat16),
            pltpu.VMEM((rows, feat), jnp.float32),
            pltpu.VMEM((feat, feat), jnp.bfloat16),
            block,
            block,
            block,
            block,
            pltpu.VMEM((feat, feat), jnp.bfloat16),
            pltpu.SemaphoreType.DMA((nb * slots,)),
            pltpu.SemaphoreType.DMA((4 * nb + 3,)),
        ],
        HB,
    )(take, start, far(pulled), far(mix), far(base), far(weight), far(cotangent))

    plane = lax.axis_size(PLANE)
    depth = lax.axis_size(DEPTH)
    mine = feat // plane
    sharers = lax.axis_size(SHARE)
    share = feat // sharers
    core = lax.axis_index("core")
    per = push_pick.shape[2]
    picks = push_pick.reshape(depth, 2, per).transpose(1, 0, 2)
    picks = jnp.where(core == 0, picks, picks[::-1]).reshape(-1, 1)
    targets = push_row.reshape(depth, 2, per)
    targets = jnp.where(core == 0, targets, targets[:, ::-1]).reshape(1, -1)

    w1 = exchange(wterm.reshape(plane, mine, feat), PLANE)
    half = jax.ShapeDtypeStruct((depth * per, feat), jnp.bfloat16)
    keep, pass_on = call(pick_kernel, "push_pick", (half, half), [VM, VM])(
        picks, layer_out
    )
    grad_layer = call(
        backward_kernel,
        "spread_backward",
        full,
        [SM, SM, VM, VM, VM],
        [
            pltpu.VMEM((nb, blk, feat), jnp.bfloat16),
            pltpu.VMEM((nb, blk, feat), jnp.float32),
        ],
    )(cols, tile_count, tiles, grad_pre, weight)

    packed = call(
        pack_kernel,
        "pack",
        jax.ShapeDtypeStruct((depth, share + 2 * per, feat), jnp.bfloat16),
        [VM, VM, VM],
    )(near(w1), near(keep), near(pass_on))
    mixed = exchange(packed, DEPTH)
    w2 = near(mixed)
    square = jax.ShapeDtypeStruct((feat, feat), jnp.bfloat16)
    grad_weight = exchange(call(finish_kernel, "finish", square, [VM])(w2), SHARE)

    passed = lax.ppermute(mixed[:, share + per :], "core", [(0, 1), (1, 0)])
    new_history = call(
        push_kernel, "push_store", jax.ShapeDtypeStruct(history.shape, jnp.bfloat16), [VM] * 4
    )(targets, w2, near(passed), history)
    return layer_out, grad_layer, grad_weight, new_history


def solution(mesh):
    fine = Mesh(mesh.devices.reshape(4, 4, 8, 2, 2), ALL)
    r2, r3 = P(ALL, None), P(ALL, None, None)
    in_specs = (r2, r2, P(), P(ALL, None, None, None), r2, P(ALL), r2, r2, r2, r3, r3, r2)
    out_specs = (r2, r2, P(), r2)
    return jax.shard_map(
        per_device, mesh=fine, in_specs=in_specs, out_specs=out_specs, check_vma=False
    )
```
